128 devices in a mesh: gx: 16 (over y_lo, x, core), gy: 4 (over z), sa: 2 (over y_hi).
Axes of the slice: x: 4, y: 4 (y_hi: 2, y_lo: 2; y = y_hi * 2 + y_lo), z: 4, core: 2. Of those that a mesh axis runs over, the one named last changes fastest.
Arguments:
- slab: float32 [2, 64, 512, 512], P(None, 'sa', 'gx', 'gy'), may hold values from -30 to 30, as said below
- factor_x: float32 [512, 256], P('gx'), may hold values from -1 to 1, as said below
- factor_y: float32 [512, 256], P('gy'), may hold values from -1 to 1, as said below
Outputs:
- gram_x: float32 [512, 512], P(('gx', 'gy', 'sa'))
- gram_y: float32 [512, 512], P('gy')
- core: float32 [2, 64, 256, 256], P(None, 'sa', 'gx', 'gy')
The draws below stay inside these ranges and needn't reach their ends.
Inputs may be any that keep to these rules, and one draw needn't show every extreme that they name: `slab`: field values of a combustion state; rows of different x cells and species differ in scale. `factor_x`: the columns are orthonormal. `factor_y`: the columns are orthonormal.
All inputs are finite; a program needn't handle non-finite values.
Results may differ from the reference program's by a relative error of at most 0.000071.
Values sent between devices are 32-bit elements; how exact they have to be, the bound alone decides.
A program may use at most 192 MiB of HBM per device.

```python
import math
import jax
import jax.numpy as jnp
from jax import lax

NX = 512
NY = 512
NS = 64
R = 256
NZ = 2


def draw_slab(key, part):
    keys = jax.random.split(jax.random.fold_in(key, 11), 3)
    low = math.log(0.3)
    high = math.log(3.0)
    row_scale = jnp.exp(jax.random.uniform(keys[0], (1, 1, NX, 1), minval=low, maxval=high))
    species_scale = jnp.exp(jax.random.uniform(keys[1], (1, NS, 1, 1), minval=low, maxval=high))
    base = jax.random.truncated_normal(keys[2], -4.0, 4.0, (NZ, NS, NX, NY))
    values = base * row_scale * species_scale
    return jnp.clip(values, -30.0, 30.0).astype(jnp.float32)


def draw_factor_x(key, part):
    matrix = jax.random.normal(jax.random.fold_in(key, 23), (NX, R))
    basis, upper = jnp.linalg.qr(matrix)
    return basis.astype(jnp.float32)


def draw_factor_y(key, part):
    matrix = jax.random.normal(jax.random.fold_in(key, 37), (NY, R))
    basis, upper = jnp.linalg.qr(matrix)
    return basis.astype(jnp.float32)


def setup_inputs(seed: int = 0) -> dict:
    seeds = jax.random.split(jax.random.key(seed), 4)
    return {
        "slab": draw_slab(jax.random.fold_in(seeds[3], 71), 0),
        "factor_x": draw_factor_x(jax.random.fold_in(seeds[3], 71), 0),
        "factor_y": draw_factor_y(jax.random.fold_in(seeds[3], 71), 0),
    }


def reference(slab, factor_x, factor_y):
    highest = lax.Precision.HIGHEST
    flat_x = jnp.transpose(slab, (2, 0, 1, 3)).reshape(NX, -1)
    gram_x = jnp.dot(flat_x.astype(jnp.float32), flat_x.T.astype(jnp.float32), precision=highest, preferred_element_type=jnp.float32) / (NY * NZ * NS)
    flat_y = jnp.transpose(slab, (3, 0, 1, 2)).reshape(NY, -1)
    gram_y = jnp.dot(flat_y.astype(jnp.float32), flat_y.T.astype(jnp.float32), precision=highest, preferred_element_type=jnp.float32) / (NX * NZ * NS)
    along_x = jnp.einsum('xa,zsxy->zsay', factor_x, slab, precision=highest)
    core = jnp.einsum('zsay,yb->zsab', along_x, factor_y, precision=highest)
    return (gram_x, gram_y, core)
```

```python
import jax
import jax.numpy as jnp
from jax import lax
from jax.sharding import PartitionSpec as P


def shards(slab, factor_x, factor_y):
    high = lax.Precision.HIGH
    z_cells, s_local, x_local, y_local = slab.shape
    n_gx, n_gy, n_sa = lax.axis_size("gx"), lax.axis_size("gy"), lax.axis_size("sa")
    x_total, y_total = x_local * n_gx, y_local * n_gy
    s_total = s_local * n_sa
    rank = factor_x.shape[1]
    a_block, b_block = rank // n_gx, rank // n_gy
    planes = z_cells * s_local
    own = planes // (n_gx * n_gy)
    fx = lax.all_gather(factor_x, "gx", axis=0, tiled=True)
    fy = lax.all_gather(factor_y, "gy", axis=0, tiled=True)
    blocks = slab.reshape(n_gx * n_gy, own, x_local, y_local)
    got = lax.all_to_all(blocks, ("gx", "gy"), split_axis=0, concat_axis=0, tiled=True)
    plane = got.reshape(n_gx, n_gy, own, x_local, y_local).transpose(2, 0, 3, 1, 4)
    plane = plane.reshape(own, x_total, y_total)

    def dot(spec, a, b):
        return jnp.einsum(spec, a, b, precision=high, preferred_element_type=jnp.float32)

    along_x = dot("pxy,xa->pay", plane, fx)
    core_planes = dot("pay,yb->pab", along_x, fy)
    core_blocks = core_planes.reshape(own, n_gx, a_block, n_gy, b_block).transpose(1, 3, 0, 2, 4)
    core_blocks = core_blocks.reshape(n_gx * n_gy, own, a_block, b_block)
    core = lax.all_to_all(core_blocks, ("gx", "gy"), split_axis=0, concat_axis=0, tiled=True)
    core = core.reshape(z_cells, s_local, a_block, b_block)
    part_x = dot("pxy,pwy->xw", plane, plane)
    part_y = dot("pxy,pxw->yw", plane, plane)
    gram_x = lax.psum_scatter(part_x, ("gx", "gy", "sa"), scatter_dimension=0, tiled=True)
    gram_x = gram_x / (y_total * z_cells * s_total)
    rows_y = lax.psum_scatter(part_y, "gy", scatter_dimension=0, tiled=True)
    gram_y = lax.psum(rows_y, ("gx", "sa")) / (x_total * z_cells * s_total)
    return (gram_x, gram_y, core)


def solution(mesh):
    in_specs = (P(None, "sa", "gx", "gy"), P("gx", None), P("gy", None))
    out_specs = (P(("gx", "gy", "sa"), None), P("gy", None), P(None, "sa", "gx", "gy"))
    return jax.shard_map(shards, mesh=mesh, in_specs=in_specs, out_specs=out_specs, check_vma=False)
```

```python
import functools

import jax
import jax.numpy as jnp
from jax import lax
from jax.experimental import pallas as pl
from jax.experimental.pallas import tpu as pltpu
from jax.sharding import PartitionSpec as P

MESH = pl.DeviceIdType.MESH
DMA = pltpu.SemaphoreType.DMA
F32 = jnp.float32
BF16 = jnp.bfloat16
VMEM = pl.BlockSpec(memory_space=pltpu.VMEM)


def loop(start, stop, body):
    def step(i, carry):
        body(i)
        return carry

    lax.fori_loop(start, stop, step, 0)


def remote(src, dst, send, recv, device):
    return pltpu.make_async_remote_copy(
        src_ref=src, dst_ref=dst, send_sem=send, recv_sem=recv, device_id=device, device_id_type=MESH
    )


def greet(devices_of, count):
    barrier = pltpu.get_barrier_semaphore()
    loop(1, count, lambda i: pl.semaphore_signal(barrier, 1, device_id=devices_of(i), device_id_type=MESH))


def exchange_kernel(
    n_gx, n_gy, slab, fx, fy, plane, fx_all, fy_all, buf_a, buf_b,
    sa1, ra1, sa2, ra2, sb1, rb1, sb2, rb2, sfx, rfx, sfy, rfy, ss, rs, local,
):
    gx, gy = lax.axis_index("gx"), lax.axis_index("gy")
    chip, core = gx // 2, lax.rem(gx, 2)
    half = slab.shape[2] // 2
    rows = 2 * half
    along_x = lambda i: lax.rem(gx + i, n_gx)
    along_y = lambda i: lax.rem(gy + i, n_gy)
    barrier = pltpu.get_barrier_semaphore()
    greet(lambda i: {"gx": along_x(i)}, n_gx)
    greet(lambda i: {"gy": along_y(i)}, n_gy)
    pl.semaphore_wait(barrier, n_gx + n_gy - 2)

    def first_a(i, slot):
        t = along_y(i)
        src = slab.at[:, t, pl.ds(0, half)]
        return remote(src, buf_a.at[slot], sa1.at[i], ra1.at[slot], {"gy": t})

    def first_b(i, slot):
        t = along_x(i)
        src = slab.at[t, :, pl.ds(half, half)]
        return remote(src, buf_b.at[slot], sb1.at[i], rb1.at[slot], {"gx": t})

    def second_a(i, owner):
        t = along_x(i)
        dst = plane.at[:, owner, pl.ds(0, half)]
        return remote(buf_a.at[:, t], dst, sa2.at[i], ra2.at[owner], {"gx": t})

    def second_b(i, owner):
        t = along_y(i)
        dst = plane.at[owner, :, pl.ds(half, half)]
        return remote(buf_b.at[:, t], dst, sb2.at[i], rb2.at[owner], {"gy": t})

    def factor_x(i, owner):
        t = lax.rem(chip + i, n_gx // 2)
        return remote(fx, fx_all.at[owner, core], sfx.at[i], rfx.at[owner], {"gx": t * 2 + core})

    def factor_y(i, owner):
        return remote(fy.at[core], fy_all.at[owner, core], sfy.at[i], rfy.at[owner], {"gy": along_y(i)})

    for i in (2, 1, 3):
        first_a(i, gy).start()
    loop(1, n_gx, lambda i: first_b(i, gx).start())
    copies = [
        pltpu.make_async_copy(slab.at[:, gy, pl.ds(0, half)], buf_a.at[gy], local.at[0]),
        pltpu.make_async_copy(slab.at[gx, :, pl.ds(half, half)], buf_b.at[gx], local.at[1]),
        pltpu.make_async_copy(fx, fx_all.at[chip, core], local.at[2]),
        pltpu.make_async_copy(fy.at[core], fy_all.at[gy, core], local.at[3]),
    ]
    for copy in copies:
        copy.start()
    copies[0].wait()
    for i in (1, 3, 2):
        first_a(i, along_y(i)).wait()
    loop(1, n_gx, lambda i: second_a(i, gx).start())
    mine_a = pltpu.make_async_copy(buf_a.at[:, gx], plane.at[:, gx, pl.ds(0, half)], local.at[4])
    mine_a.start()
    copies[1].wait()
    loop(1, n_gx, lambda i: first_b(i, along_x(i)).wait())
    for i in (2, 1, 3):
        second_b(i, gy).start()
    mine_b = pltpu.make_async_copy(buf_b.at[:, gy], plane.at[gy, :, pl.ds(half, half)], local.at[5])
    mine_b.start()
    for i in (2, 1, 3):
        factor_y(i, gy).start()
    loop(1, n_gx // 2, lambda i: factor_x(i, chip).start())
    copies[2].wait()
    copies[3].wait()
    for i in (1, 3, 2):
        factor_y(i, along_y(i)).wait()
    sibling = {"gx": chip * 2 + 1 - core}
    share_y = remote(fy_all.at[:, core], fy_all.at[:, core], ss.at[0], rs.at[0], sibling)
    share_y.start()
    loop(1, n_gx // 2, lambda i: factor_x(i, lax.rem(chip + i, n_gx // 2)).wait())
    share_x = remote(fx_all.at[:, core], fx_all.at[:, core], ss.at[1], rs.at[1], sibling)
    share_x.start()
    loop(1, n_gx, lambda i: second_a(i, along_x(i)).wait())
    for i in (1, 3, 2):
        second_b(i, along_y(i)).wait()
    mine_a.wait()
    mine_b.wait()
    remote(fy_all.at[:, core], fy_all.at[:, 1 - core], ss.at[0], rs.at[0], sibling).wait()
    remote(fx_all.at[:, core], fx_all.at[:, 1 - core], ss.at[1], rs.at[1], sibling).wait()


def exchange(slab, fx, fy, n_gx, n_gy):
    x_local, y_local = slab.shape[2:]
    rank = fx.shape[1]
    half = x_local // 2
    blocks = slab.reshape(n_gx, n_gy, x_local, y_local)
    plane, fx_all, fy_all = pl.pallas_call(
        functools.partial(exchange_kernel, n_gx, n_gy),
        out_shape=(
            jax.ShapeDtypeStruct((n_gy, n_gx, x_local, y_local), F32),
            jax.ShapeDtypeStruct((n_gx // 2, 2, x_local, rank), F32),
            jax.ShapeDtypeStruct((n_gy, 2, y_local // 2, rank), F32),
        ),
        in_specs=[VMEM] * 3,
        out_specs=(VMEM,) * 3,
        scratch_shapes=[
            pltpu.VMEM((n_gy, n_gx, half, y_local), F32),
            pltpu.VMEM((n_gx, n_gy, half, y_local), F32),
            DMA((n_gy,)), DMA((n_gy,)), DMA((n_gx,)), DMA((n_gx,)),
            DMA((n_gx,)), DMA((n_gx,)), DMA((n_gy,)), DMA((n_gy,)),
            DMA((n_gx // 2,)), DMA((n_gx // 2,)), DMA((n_gy,)), DMA((n_gy,)),
            DMA((2,)), DMA((2,)), DMA((6,)),
        ],
        compiler_params=pltpu.CompilerParams(collective_id=0, has_side_effects=True, vmem_limit_bytes=32 << 20),
        name="exchange",
    )(blocks, fx, fy.reshape(2, y_local // 2, rank))
    return (
        plane.reshape(n_gy, n_gx * x_local, y_local),
        fx_all.reshape(n_gx * x_local, rank),
        fy_all.reshape(n_gy * y_local, rank),
    )


def split(value):
    high = value.astype(BF16)
    return high, (value - high.astype(F32)).astype(BF16)


def dot3(a, b, dims):
    (a_high, a_low), (b_high, b_low) = a, b
    dot = lambda p, q: lax.dot_general(p, q, (dims, ((), ())), preferred_element_type=F32)
    return dot(a_high, b_low) + dot(a_low, b_high) + dot(a_high, b_high)


def local_kernel(n_gx, n_gy, plane, fx, fy, grams, tiles):
    whole = jnp.concatenate([plane[g] for g in range(n_gy)], axis=1)
    p = split(whole)
    grams[0] = dot3(p, p, ((1,), (1,)))
    grams[1] = dot3(p, p, ((0,), (0,)))
    q = split(dot3(p, split(fy[...]), ((1,), (0,))))
    core = dot3(split(fx[...]), q, ((0,), (0,)))
    a_half = core.shape[0] // n_gx // 2
    b_block = core.shape[1] // n_gy
    core = core.reshape(n_gx, 2, a_half, core.shape[1])
    low = core[:, 0].reshape(n_gx * a_half, -1)
    high = core[:, 1].reshape(n_gx * a_half, -1)
    lane = lax.broadcasted_iota(jnp.int32, (n_gx * a_half, 2 * b_block), 1)
    for g in range(n_gy):
        j = g // 2 * 2 * b_block
        left, right = low[:, j : j + 2 * b_block], high[:, j : j + 2 * b_block]
        if g % 2 == 0:
            right = pltpu.roll(right, b_block, 1)
        else:
            left = pltpu.roll(left, b_block, 1)
        tiles[g] = jnp.where(lane < b_block, left, right)


def local_work(plane, fx, fy, n_gx, n_gy):
    x_total, y_total = fx.shape[0], fy.shape[0]
    rank = fx.shape[1]
    return pl.pallas_call(
        functools.partial(local_kernel, n_gx, n_gy),
        out_shape=(
            jax.ShapeDtypeStruct((2, x_total, y_total), F32),
            jax.ShapeDtypeStruct((n_gy, rank // 2, 2 * rank // n_gy), F32),
        ),
        in_specs=[VMEM] * 3,
        out_specs=(VMEM,) * 2,
        compiler_params=pltpu.CompilerParams(vmem_limit_bytes=40 << 20),
        name="local_work",
    )(plane, fx, fy)


def reduce_kernel(
    scale, grams, tiles, gram_x, gram_y, core_out,
    total, got0, got1, part1, got2, part2, got3, part3, last, mid, packed,
    s0, r0, s1, r1, s2, r2, s3, r3, s4, r4, sc1, rc1, sc2, rc2, local,
):
    gx, gy, sa = lax.axis_index("gx"), lax.axis_index("gy"), lax.axis_index("sa")
    n_gx, n_gy = 16, 4
    core = lax.rem(gx, 2)
    x = lax.rem(gx // 2, 4)
    y_lo = gx // 8
    y = sa * 2 + y_lo
    step = lambda v, i: lax.rem(v + i, 4)

    def chip_at(to_x, to_y, to_core):
        return {"gx": lax.rem(to_y, 2) * 8 + to_x * 2 + to_core, "sa": to_y // 2}

    def plane_at(i):
        d = lax.rem(sa * n_gx + gx + i, 2 * n_gx)
        return {"gx": lax.rem(d, n_gx), "sa": d // n_gx}

    at_x = lambda i: chip_at(step(x, i), y, core)
    at_y = lambda i: chip_at(x, step(y, i), core)
    at_z = lambda i: {"gy": step(gy, i)}
    sibling = {"gx": gx + 1 - 2 * core}
    barrier = pltpu.get_barrier_semaphore()
    greet(plane_at, 2 * n_gx)
    greet(at_z, n_gy)
    pl.semaphore_wait(barrier, 2 * n_gx - 1 + n_gy - 1)

    swap = remote(grams.at[1 - core], got0, s0, r0, sibling)
    swap.start()
    out1 = lambda i, slot: remote(tiles.at[step(gy, i)], mid.at[slot], sc1.at[i], rc1.at[slot], at_z(i))
    for i in (2, 1, 3):
        out1(i, gy).start()
    mine = pltpu.make_async_copy(tiles.at[gy], mid.at[gy], local.at[0])
    mine.start()
    swap.wait()
    total[...] = grams[core] + got0[...]

    by_z = total.reshape(16, 4, 8, 512)
    by_x = total.reshape(4, 4, 4, 8, 512)
    got1_x = got1.reshape(4, 4, 4, 8, 512)
    part1_x = part1.reshape(4, 4, 8, 512)
    part1_z = part1.reshape(2, 4, 2, 8, 512)
    got2_z = got2.reshape(4, 2, 2, 8, 512)
    part2_x = part2.reshape(2, 2, 8, 512)

    def z1(i, slot):
        return remote(by_z.at[:, step(gy, i)], got1.at[slot], s1.at[i], r1.at[slot], at_z(i))

    def x1(i, slot):
        return remote(by_x.at[:, step(x, i)], got1_x.at[slot], s1.at[i], r1.at[slot], at_x(i))

    def x2(i, slot):
        return remote(part1_z.at[:, step(x, i)], got2_z.at[slot], s2.at[i], r2.at[slot], at_x(i))

    def z2(i, slot):
        return remote(part1_x.at[step(gy, i)], got2.at[slot], s2.at[i], r2.at[slot], at_z(i))

    def y3(i, slot):
        return remote(part2_x.at[lax.rem(step(y, i), 2)], got3.at[slot], s3.at[i], r3.at[slot], at_y(i))

    def y3_one(i, slot):
        return remote(part2.at[step(y, i)], got3.at[slot, 0], s3.at[i], r3.at[slot], at_y(i))

    def send(copy, own):
        for i in (2, 1, 3):
            copy(i, own).start()

    def receive(copy, own):
        for i in (1, 3, 2):
            copy(i, step(own, i)).wait()

    @pl.when(core == 0)
    def _():
        send(z1, gy)

    @pl.when(core == 1)
    def _():
        send(x1, x)

    mine.wait()
    for i in (1, 3, 2):
        out1(i, step(gy, i)).wait()
    mid4 = mid.reshape(n_gy, n_gx, 8, 128)

    def out2(i, owner):
        t = lax.rem(gx + i, n_gx)
        return remote(mid4.at[:, t], packed.at[owner], sc2.at[i], rc2.at[owner], {"gx": t})

    loop(1, n_gx, lambda i: out2(i, gx).start())
    mine2 = pltpu.make_async_copy(mid4.at[:, gx], packed.at[gx], local.at[1])
    mine2.start()

    @pl.when(core == 0)
    def _():
        receive(z1, gy)
        part1[...] = by_z[:, gy] + ((got1[step(gy, 1)] + got1[step(gy, 3)]) + got1[step(gy, 2)])
        send(x2, x)
        receive(x2, x)
        part2_x[...] = part1_z[:, x] + ((got2_z[step(x, 1)] + got2_z[step(x, 3)]) + got2_z[step(x, 2)])
        send(y3, y)
        receive(y3, y)
        rows = part2_x[y_lo] + ((got3[step(y, 1)] + got3[step(y, 3)]) + got3[step(y, 2)])
        part3[...] = rows * scale
        to_sibling = remote(part3.at[1], last, s4.at[0], r4.at[16], sibling)
        to_sibling.start()
        gram_x[...] = jnp.where(sa == 0, part3[0, 0:4], part3[0, 4:8])
        to_sibling.wait_send()

    @pl.when(core == 1)
    def _():
        receive(x1, x)
        part1_x[...] = by_x[:, x] + ((got1_x[step(x, 1)] + got1_x[step(x, 3)]) + got1_x[step(x, 2)])
        send(z2, gy)
        receive(z2, gy)
        part2[...] = part1_x[gy] + ((got2[step(gy, 1)] + got2[step(gy, 3)]) + got2[step(gy, 2)])
        send(y3_one, y)
        receive(y3_one, y)
        rows = part2[y] + ((got3[step(y, 1), 0] + got3[step(y, 3), 0]) + got3[step(y, 2), 0])
        gram_y[x, y] = rows * scale

        def share(i):
            return remote(gram_y.at[x, y], gram_y.at[x, y], s4.at[i], r4.at[x * 4 + y], plane_at(i))

        loop(1, 2 * n_gx, lambda i: share(i).start())
        remote(part3.at[1], last, s4.at[0], r4.at[16], sibling).wait_recv()
        gram_x[...] = jnp.where(sa == 0, last[0:4], last[4:8])
        loop(1, 2 * n_gx, lambda i: share(i).wait_send())

    mine2.wait()
    loop(1, n_gx, lambda i: out2(i, lax.rem(gx + i, n_gx)).wait())
    tile = packed[...].reshape(n_gx * n_gy, 8, 128)
    core_out[:, 0:8, :] = tile[:, :, 0:64]
    core_out[:, 8:16, :] = tile[:, :, 64:128]

    def arrived(j):
        piece = gram_y.at[j // 4, lax.rem(j, 4)]
        remote(piece, piece, s4.at[0], r4.at[j], sibling).wait_recv()

    mine_j = x * 4 + y

    def take(i):
        arrived(lax.rem(mine_j + i, 16))

    loop(1, 16, take)

    @pl.when(core == 0)
    def _():
        arrived(mine_j)


def reduce_all(grams, tiles, n_gx, n_gy, scale):
    n = grams.shape[1]
    return pl.pallas_call(
        functools.partial(reduce_kernel, scale),
        out_shape=(
            jax.ShapeDtypeStruct((4, n), F32),
            jax.ShapeDtypeStruct((4, 4, 8, n), F32),
            jax.ShapeDtypeStruct((n_gx * n_gy, 16, 64), F32),
        ),
        in_specs=[VMEM] * 2,
        out_specs=(VMEM,) * 3,
        scratch_shapes=[
            pltpu.VMEM((n, n), F32),
            pltpu.VMEM((n, n), F32),
            pltpu.VMEM((4, 16, 8, n), F32),
            pltpu.VMEM((16, 8, n), F32),
            pltpu.VMEM((4, 4, 8, n), F32),
            pltpu.VMEM((4, 8, n), F32),
            pltpu.VMEM((4, 2, 8, n), F32),
            pltpu.VMEM((2, 8, n), F32),
            pltpu.VMEM((8, n), F32),
            pltpu.VMEM((n_gy, 128, 128), F32),
            pltpu.VMEM((n_gx, n_gy, 8, 128), F32),
            DMA(()), DMA(()), DMA((4,)), DMA((4,)), DMA((4,)), DMA((4,)), DMA((4,)), DMA((4,)),
            DMA((32,)), DMA((17,)), DMA((4,)), DMA((4,)), DMA((16,)), DMA((16,)), DMA((2,)),
        ],
        compiler_params=pltpu.CompilerParams(collective_id=1, has_side_effects=True, vmem_limit_bytes=40 << 20),
        name="reduce_all",
    )(grams, tiles)


def shards(slab, factor_x, factor_y):
    z_cells, s_local, x_local, y_local = slab.shape
    n_gx, n_gy, n_sa = lax.axis_size("gx"), lax.axis_size("gy"), lax.axis_size("sa")
    scale = 1.0 / (y_local * n_gy * z_cells * s_local * n_sa)
    plane, fx, fy = exchange(slab, factor_x, factor_y, n_gx, n_gy)
    grams, tiles = local_work(plane, fx, fy, n_gx, n_gy)
    gram_x, gram_y, core = reduce_all(grams, tiles, n_gx, n_gy, scale)
    rank = factor_x.shape[1]
    core = core.reshape(z_cells, s_local, rank // n_gx, rank // n_gy)
    return gram_x, gram_y.reshape(y_local, -1), core


def solution(mesh):
    in_specs = (P(None, "sa", "gx", "gy"), P("gx", None), P("gy", None))
    out_specs = (P(("gx", "gy", "sa"), None), P("gy", None), P(None, "sa", "gx", "gy"))
    return jax.shard_map(shards, mesh=mesh, in_specs=in_specs, out_specs=out_specs, check_vma=False)
```

```python
import functools

import jax
import jax.numpy as jnp
from jax import lax
from jax.experimental import pallas as pl
from jax.experimental.pallas import tpu as pltpu
from jax.sharding import PartitionSpec as P

MESH = pl.DeviceIdType.MESH
DMA = pltpu.SemaphoreType.DMA
F32 = jnp.float32
BF16 = jnp.bfloat16
VMEM = pl.BlockSpec(memory_space=pltpu.VMEM)
HBM = pl.BlockSpec(memory_space=pltpu.HBM)
ORDER = (2, 1, 3)


def loop(start, stop, body):
    def step(i, carry):
        body(i)
        return carry

    lax.fori_loop(start, stop, step, 0)


def remote(src, dst, send, recv, device):
    return pltpu.make_async_remote_copy(
        src_ref=src, dst_ref=dst, send_sem=send, recv_sem=recv, device_id=device, device_id_type=MESH
    )


def greet(devices_of, count):
    barrier = pltpu.get_barrier_semaphore()
    loop(1, count, lambda i: pl.semaphore_signal(barrier, 1, device_id=devices_of(i), device_id_type=MESH))


def split(value):
    high = value.astype(BF16)
    return high, (value - high.astype(F32)).astype(BF16)


def dot3(a, b, dims):
    (a_high, a_low), (b_high, b_low) = a, b
    dot = lambda p, q: lax.dot_general(p, q, (dims, ((), ())), preferred_element_type=F32)
    return dot(a_high, b_low) + dot(a_low, b_high) + dot(a_high, b_high)


def tucker_kernel(
    scale, slab, fx, fy, gram_x, gram_y_t, core_tiles,
    buf_a, buf_b, plane, fx_all, fy_all, p_high, p_low, to_sib, got0, total, got1, part1, got2, part2, last, tiles, mid,
    sa1, ra1, sa2, ra2, sb1, rb1, sb2, rb2, sfx, rfx, sfy, rfy, ss, rs,
    s0, r0, s1, r1, s2, r2, s4, r4, sc1, rc1, sc2, rc2, local,
):
    gx, gy, sa = lax.axis_index("gx"), lax.axis_index("gy"), lax.axis_index("sa")
    n_gx, n_gy = 16, 4
    chip, core = gx // 2, lax.rem(gx, 2)
    x, y_lo = lax.rem(chip, 4), chip // 4
    y = sa * 2 + y_lo
    half = 16
    step = lambda v, i: lax.rem(v + i, 4)
    along_x = lambda i: lax.rem(gx + i, n_gx)
    along_y = lambda i: lax.rem(gy + i, n_gy)
    sibling = {"gx": gx + 1 - 2 * core}

    def chip_at(to_x, to_y, to_z):
        return {"gx": lax.rem(to_y, 2) * 8 + to_x * 2 + core, "gy": to_z, "sa": to_y // 2}

    barrier = pltpu.get_barrier_semaphore()
    greet(lambda i: {"gx": along_x(i)}, n_gx)
    greet(lambda i: {"gy": along_y(i)}, n_gy)
    loop(0, 8, lambda i: pl.semaphore_signal(
        barrier, 1, device_id={"gx": i * 2 + core, "sa": 1 - sa}, device_id_type=MESH))

    @pl.when(core == 1)
    def _():
        for i in (1, 2, 3):
            for j in (1, 2, 3):
                pl.semaphore_signal(barrier, 1, device_id=chip_at(x, step(y, i), step(gy, j)), device_id_type=MESH)

    pl.semaphore_wait(barrier, n_gx + n_gy - 2 + 8 + 9 * core)

    def first_a(i, slot):
        t = along_y(i)
        return remote(slab.at[:, t, pl.ds(0, half)], buf_a.at[slot], sa1.at[i], ra1.at[slot], {"gy": t})

    def first_b(i, slot):
        t = along_x(i)
        return remote(slab.at[t, :, pl.ds(half, half)], buf_b.at[slot], sb1.at[i], rb1.at[slot], {"gx": t})

    def second_a(i, owner):
        t = along_x(i)
        dst = plane.at[:, owner, pl.ds(0, half)]
        return remote(buf_a.at[:, t], dst, sa2.at[i], ra2.at[owner], {"gx": t})

    def second_b(i, owner):
        t = along_y(i)
        dst = plane.at[owner, :, pl.ds(half, half)]
        return remote(buf_b.at[:, t], dst, sb2.at[i], rb2.at[owner], {"gy": t})

    def factor_x(i, owner):
        t = lax.rem(chip + i, n_gx // 2)
        return remote(fx, fx_all.at[owner, core], sfx.at[i], rfx.at[owner], {"gx": t * 2 + core})

    def factor_y(i, owner):
        return remote(fy.at[core], fy_all.at[owner, core], sfy.at[i], rfy.at[owner], {"gy": along_y(i)})

    def share(all_ref, k, side):
        return remote(all_ref.at[:, core], all_ref.at[:, side], ss.at[k], rs.at[k], sibling)

    for i in ORDER:
        first_a(i, gy).start()
    loop(1, n_gx, lambda i: first_b(i, gx).start())
    copies = [
        pltpu.make_async_copy(slab.at[:, gy, pl.ds(0, half)], buf_a.at[gy], local.at[0]),
        pltpu.make_async_copy(slab.at[gx, :, pl.ds(half, half)], buf_b.at[gx], local.at[1]),
        pltpu.make_async_copy(fx, fx_all.at[chip, core], local.at[2]),
        pltpu.make_async_copy(fy.at[core], fy_all.at[gy, core], local.at[3]),
    ]
    for copy in copies:
        copy.start()
    copies[0].wait()
    for i in (1, 3, 2):
        first_a(i, along_y(i)).wait()
    loop(1, n_gx, lambda i: second_a(i, gx).start())
    mine_a = pltpu.make_async_copy(buf_a.at[:, gx], plane.at[:, gx, pl.ds(0, half)], local.at[4])
    mine_a.start()
    copies[1].wait()
    loop(1, n_gx, lambda i: first_b(i, along_x(i)).wait())
    for i in ORDER:
        second_b(i, gy).start()
    mine_b = pltpu.make_async_copy(buf_b.at[:, gy], plane.at[gy, :, pl.ds(half, half)], local.at[5])
    mine_b.start()
    for i in ORDER:
        factor_y(i, gy).start()
    loop(1, n_gx // 2, lambda i: factor_x(i, chip).start())
    loop(1, n_gx, lambda i: second_a(i, along_x(i)).wait())
    for i in (1, 3, 2):
        second_b(i, along_y(i)).wait()
    mine_a.wait()
    mine_b.wait()

    for g in range(n_gy):
        p_high[g], p_low[g] = split(plane[g].reshape(512, 128))
    joined = lambda ref: jnp.concatenate([ref[g] for g in range(n_gy)], axis=1)

    def x_rows(q):
        rows = plane[:, :, pl.ds(pl.multiple_of(q * 8, 8), 8), :].reshape(n_gy, 128, 128)
        rows = jnp.concatenate([rows[g] for g in range(n_gy)], axis=1)
        return dot3(split(rows), (joined(p_high), joined(p_low)), ((1,), (1,)))

    def y_rows(q):
        return dot3((p_high[q], p_low[q]), (joined(p_high), joined(p_low)), ((0,), (0,)))

    def x_part(i, slot):
        t = step(gy, i)
        return remote(total.at[t], got1.at[slot], s1.at[i], r1.at[slot], {"gy": t})

    def y_part(i, slot):
        t = step(x, i)
        return remote(total.at[t], got1.at[slot], s1.at[i], r1.at[slot], chip_at(t, y, gy))

    def swap(q):
        return remote(to_sib.at[q], got0.at[q], s0.at[q], r0.at[q], sibling)

    def grams(theirs, their_q, mine, my_q, part):
        for i in (2, 1, 3, 0):
            q = step(their_q, i)
            to_sib[q] = theirs(q)
            swap(q).start()
        for i in (2, 1, 3, 0):
            q = step(my_q, i)
            value = mine(q)
            swap(q).wait_recv()
            total[q] = value + got0[q]
            if i:
                part(i, my_q).start()

    @pl.when(core == 0)
    def _():
        grams(y_rows, x, x_rows, gy, x_part)

    @pl.when(core == 1)
    def _():
        grams(x_rows, gy, y_rows, x, y_part)

    copies[2].wait()
    copies[3].wait()
    for i in (1, 3, 2):
        factor_y(i, along_y(i)).wait()
    share(fy_all, 0, core).start()
    loop(1, n_gx // 2, lambda i: factor_x(i, lax.rem(chip + i, n_gx // 2)).wait())
    share(fx_all, 1, core).start()
    share(fy_all, 0, 1 - core).wait()
    whole = (joined(p_high), joined(p_low))
    inner = split(dot3(whole, split(fy_all[...].reshape(512, 256)), ((1,), (0,))))
    share(fx_all, 1, 1 - core).wait()
    product = dot3(split(fx_all[...].reshape(512, 256)), inner, ((0,), (0,)))
    product = product.reshape(n_gx, 2, 8, 256)
    upper, lower = product[:, 0].reshape(128, 256), product[:, 1].reshape(128, 256)
    lane = lax.broadcasted_iota(jnp.int32, (128, 128), 1)
    for g in range(n_gy):
        j = g // 2 * 128
        left, right = upper[:, j : j + 128], lower[:, j : j + 128]
        if g % 2 == 0:
            right = pltpu.roll(right, 64, 1)
        else:
            left = pltpu.roll(left, 64, 1)
        tiles[g] = jnp.where(lane < 64, left, right)

    def out1(i, slot):
        t = along_y(i)
        return remote(tiles.at[t], mid.at[slot], sc1.at[i], rc1.at[slot], {"gy": t})

    for i in ORDER:
        out1(i, gy).start()
    mine1 = pltpu.make_async_copy(tiles.at[gy], mid.at[gy], local.at[0])
    mine1.start()

    def x_piece(i, slot):
        j = lax.rem(x * 4 + y + i, 16)
        to_x, to_y = j // 4, lax.rem(j, 4)
        src = part1.at[(lax.rem(to_y, 2) * 4 + to_x) * 2 + to_y // 2]
        return remote(src, got2.at[slot], s2.at[i], r2.at[slot], chip_at(to_x, to_y, gy))

    def y_piece(i, slot):
        j = lax.rem(gy * 4 + y + i, 16)
        to_z, to_y = j // 4, lax.rem(j, 4)
        return remote(part1.at[j], got2.at[slot], s2.at[i], r2.at[slot], chip_at(x, to_y, to_z))

    def to_plane(i, slot):
        j = lax.rem(x * 4 + y + i, 16)
        dst = gram_y_t.at[slot]
        return remote(dst, dst, s4.at[i], r4.at[slot], chip_at(j // 4, lax.rem(j, 4), gy))

    def sum_parts(part, own):
        for i in (1, 3, 2):
            part(i, step(own, i)).wait()
        return (total[own] + got1[step(own, 2)]) + (got1[step(own, 1)] + got1[step(own, 3)])

    @pl.when(core == 0)
    def _():
        rows = sum_parts(x_part, gy).reshape(8, 2, 8, 512)
        even, odd = rows[:, 0].reshape(64, 512), rows[:, 1].reshape(64, 512)
        sub = lax.rem(lax.broadcasted_iota(jnp.int32, (64, 512), 0), 8)
        low = jnp.where(sub < 4, even, pltpu.roll(odd, 4, 0)).reshape(8, 8, 512)
        high = jnp.where(sub < 4, pltpu.roll(even, 60, 0), odd).reshape(8, 8, 512)
        by_tile = part1.reshape(8, 2, 4, 8, 128)
        for t in range(4):
            by_tile[:, 0, t] = low[:, :, 128 * t : 128 * t + 128]
            by_tile[:, 1, t] = high[:, :, 128 * t : 128 * t + 128]
        me = x * 4 + y
        loop(1, 16, lambda i: x_piece(i, me).start())

    @pl.when(core == 1)
    def _():
        rows = sum_parts(y_part, x)
        for z in range(4):
            part1[4 * z : 4 * z + 4] = rows[:, 128 * z : 128 * z + 128].reshape(4, 32, 128)
        me = gy * 4 + y
        loop(1, 16, lambda i: y_piece(i, me).start())

    mine1.wait()
    for i in (1, 3, 2):
        out1(i, along_y(i)).wait()
    mid4 = mid.reshape(n_gy, n_gx, 8, 128)

    def out2(i, owner):
        t = along_x(i)
        return remote(mid4.at[:, t], core_tiles.at[owner], sc2.at[i], rc2.at[owner], {"gx": t})

    loop(1, n_gx, lambda i: out2(i, gx).start())
    mine2 = pltpu.make_async_copy(mid4.at[:, gx], core_tiles.at[gx], local.at[1])
    mine2.start()

    to_sibling = remote(part2, last, s4.at[0], r4.at[16], sibling)
    all_rows = remote(gram_y_t, gram_y_t, s4.at[0], r4.at[17], sibling)

    @pl.when(core == 0)
    def _():
        me = x * 4 + y
        loop(1, 16, lambda i: x_piece(i, lax.rem(me + i, 16)).wait())
        got2[me] = part1[(y_lo * 4 + x) * 2 + sa]
        part2[...] = jnp.sum(got2[...], axis=0) * scale
        to_sibling.start()
        for t in range(4):
            gram_x[:, 128 * t : 128 * t + 128] = part2[8 * t : 8 * t + 4]
        to_sibling.wait_send()
        all_rows.wait_recv()

    @pl.when(core == 1)
    def _():
        me = gy * 4 + y
        loop(1, 16, lambda i: y_piece(i, lax.rem(me + i, 16)).wait())
        got2[me] = part1[me]
        here = x * 4 + y
        gram_y_t[here] = jnp.sum(got2[...], axis=0) * scale
        loop(1, 16, lambda i: to_plane(i, here).start())
        to_sibling.wait_recv()
        for t in range(4):
            gram_x[:, 128 * t : 128 * t + 128] = last[8 * t + 4 : 8 * t + 8]
        loop(1, 16, lambda i: to_plane(i, lax.rem(here + i, 16)).wait())
        all_rows.start()
        all_rows.wait_send()

    mine2.wait()
    loop(1, n_gx, lambda i: out2(i, along_x(i)).wait())
    loop(0, 4, lambda q: swap(q).wait_send())


def finish_kernel(gx_in, gy_in, core_in, gx_out, gy_out, core_out):
    gx_out[...] = gx_in[...]
    gy_out[...] = gy_in[...].reshape(512, 128).T
    tile = core_in[...].reshape(64, 8, 128)
    core_out[:, 0:8, :] = tile[:, :, 0:64]
    core_out[:, 8:16, :] = tile[:, :, 64:128]


def shards(slab, factor_x, factor_y):
    z_cells, s_local, x_local, y_local = slab.shape
    n_gx, n_gy, n_sa = lax.axis_size("gx"), lax.axis_size("gy"), lax.axis_size("sa")
    scale = 1.0 / (y_local * n_gy * z_cells * s_local * n_sa)
    rank = factor_x.shape[1]
    vmem = pltpu.VMEM
    results = pl.pallas_call(
        functools.partial(tucker_kernel, scale),
        out_shape=(
            jax.ShapeDtypeStruct((4, 512), F32),
            jax.ShapeDtypeStruct((16, 32, 128), F32),
            jax.ShapeDtypeStruct((n_gx, n_gy, 8, 128), F32),
        ),
        in_specs=[HBM] * 3,
        out_specs=(VMEM,) * 3,
        scratch_shapes=[
            vmem((4, 16, 16, 128), F32), vmem((16, 4, 16, 128), F32), vmem((4, 16, 32, 128), F32),
            vmem((8, 2, 32, 256), F32), vmem((4, 2, 64, 256), F32),
            vmem((4, 512, 128), BF16), vmem((4, 512, 128), BF16),
            vmem((4, 128, 512), F32), vmem((4, 128, 512), F32), vmem((4, 128, 512), F32), vmem((4, 128, 512), F32),
            vmem((16, 32, 128), F32), vmem((16, 32, 128), F32), vmem((32, 128), F32), vmem((32, 128), F32),
            vmem((4, 128, 128), F32), vmem((4, 128, 128), F32),
            DMA((4,)), DMA((4,)), DMA((16,)), DMA((16,)), DMA((16,)), DMA((16,)), DMA((4,)), DMA((4,)),
            DMA((8,)), DMA((8,)), DMA((4,)), DMA((4,)), DMA((2,)), DMA((2,)),
            DMA((4,)), DMA((4,)), DMA((4,)), DMA((4,)), DMA((16,)), DMA((16,)), DMA((16,)), DMA((18,)),
            DMA((4,)), DMA((4,)), DMA((16,)), DMA((16,)), DMA((6,)),
        ],
        compiler_params=pltpu.CompilerParams(collective_id=0, has_side_effects=True, vmem_limit_bytes=56 << 20),
        name="tucker",
    )(
        slab.reshape(n_gx, n_gy, x_local, y_local), factor_x, factor_y.reshape(2, y_local // 2, rank)
    )
    gram_x, gram_y, core = pl.pallas_call(
        finish_kernel,
        out_shape=(
            jax.ShapeDtypeStruct((4, 512), F32),
            jax.ShapeDtypeStruct((128, 512), F32),
            jax.ShapeDtypeStruct((64, 16, 64), F32),
        ),
        in_specs=[VMEM] * 3,
        out_specs=(VMEM,) * 3,
        name="finish",
    )(*results)
    return gram_x, gram_y, core.reshape(z_cells, s_local, rank // n_gx, rank // n_gy)


def solution(mesh):
    in_specs = (P(None, "sa", "gx", "gy"), P("gx", None), P("gy", None))
    out_specs = (P(("gx", "gy", "sa"), None), P("gy", None), P(None, "sa", "gx", "gy"))
    return jax.shard_map(shards, mesh=mesh, in_specs=in_specs, out_specs=out_specs, check_vma=False)
```

```python
import functools

import jax
import jax.numpy as jnp
from jax import lax
from jax.experimental import pallas as pl
from jax.experimental.pallas import tpu as pltpu
from jax.sharding import PartitionSpec as P

MESH = pl.DeviceIdType.MESH
DMA = pltpu.SemaphoreType.DMA
F32 = jnp.float32
BF16 = jnp.bfloat16
VMEM = pl.BlockSpec(memory_space=pltpu.VMEM)
HBM = pl.BlockSpec(memory_space=pltpu.HBM)
ORDER = (2, 1, 3)


def loop(start, stop, body):
    def step(i, carry):
        body(i)
        return carry

    lax.fori_loop(start, stop, step, 0)


def remote(src, dst, send, recv, device):
    return pltpu.make_async_remote_copy(
        src_ref=src, dst_ref=dst, send_sem=send, recv_sem=recv, device_id=device, device_id_type=MESH
    )


def greet(devices_of, count):
    barrier = pltpu.get_barrier_semaphore()
    loop(1, count, lambda i: pl.semaphore_signal(barrier, 1, device_id=devices_of(i), device_id_type=MESH))


def split(value):
    high = value.astype(BF16)
    return high, (value - high.astype(F32)).astype(BF16)


def dot3(a, b, dims):
    (a_high, a_low), (b_high, b_low) = a, b
    dot = lambda p, q: lax.dot_general(p, q, (dims, ((), ())), preferred_element_type=F32)
    return dot(a_high, b_low) + dot(a_low, b_high) + dot(a_high, b_high)


def tucker_kernel(
    scale, slab, fx, fy, gram_x, gram_y_t, core_tiles,
    buf_a, buf_b, plane, fx_all, fy_all, p_high, p_low, to_sib, got0, total, got1, part1, got2, part2, last, tiles, mid,
    sa1, ra1, sa2, ra2, sb1, rb1, sb2, rb2, sfx, rfx, sfy, rfy, ss, rs,
    s0, r0, s1, r1, s2, r2, s4, r4, sc1, rc1, sc2, rc2, local,
):
    gx, gy, sa = lax.axis_index("gx"), lax.axis_index("gy"), lax.axis_index("sa")
    n_gx, n_gy = 16, 4
    chip, core = gx // 2, lax.rem(gx, 2)
    x, y_lo = lax.rem(chip, 4), chip // 4
    y = sa * 2 + y_lo
    half = 16
    step = lambda v, i: lax.rem(v + i, 4)
    along_x = lambda i: lax.rem(gx + i, n_gx)
    along_y = lambda i: lax.rem(gy + i, n_gy)
    sibling = {"gx": gx + 1 - 2 * core}

    def chip_at(to_x, to_y, to_z):
        return {"gx": lax.rem(to_y, 2) * 8 + to_x * 2 + core, "gy": to_z, "sa": to_y // 2}

    barrier = pltpu.get_barrier_semaphore()
    greet(lambda i: {"gx": along_x(i)}, n_gx)
    greet(lambda i: {"gy": along_y(i)}, n_gy)
    loop(0, 8, lambda i: pl.semaphore_signal(
        barrier, 1, device_id={"gx": i * 2 + core, "sa": 1 - sa}, device_id_type=MESH))

    @pl.when(core == 1)
    def _():
        for i in (1, 2, 3):
            for j in (1, 2, 3):
                pl.semaphore_signal(barrier, 1, device_id=chip_at(x, step(y, i), step(gy, j)), device_id_type=MESH)

    pl.semaphore_wait(barrier, n_gx + n_gy - 2 + 8 + 9 * core)

    def first_a(p, i):
        t = along_y(i)
        return remote(slab.at[:, t, pl.ds(8 * p, 8)], buf_a.at[p, gy], sa1.at[p], ra1.at[p], {"gy": t})

    def first_b(p, i):
        t = along_x(i)
        return remote(slab.at[t, :, pl.ds(half + 8 * p, 8)], buf_b.at[p, gx], sb1.at[p], rb1.at[p], {"gx": t})

    def second_a(p, i):
        t = along_x(i)
        dst = plane.at[:, gx, pl.ds(8 * p, 8)]
        return remote(buf_a.at[p, :, t], dst, sa2.at[p], ra2.at[p], {"gx": t})

    def second_b(p, i):
        t = along_y(i)
        dst = plane.at[gy, :, pl.ds(half + 8 * p, 8)]
        return remote(buf_b.at[p, :, t], dst, sb2.at[p], rb2.at[p], {"gy": t})

    def bytes_of(ref, send, recv):
        return remote(ref, ref, send, recv, sibling)

    three = lambda send, recv: bytes_of(buf_a.at[0, pl.ds(0, 3)], send, recv)
    fifteen = lambda send, recv: bytes_of(buf_b.at[0, pl.ds(0, 15)], send, recv)

    def factor_x(i, owner):
        t = lax.rem(chip + i, n_gx // 2)
        return remote(fx, fx_all.at[owner, core], sfx.at[i], rfx.at[owner], {"gx": t * 2 + core})

    def factor_y(i, owner):
        return remote(fy.at[core], fy_all.at[owner, core], sfy.at[i], rfy.at[owner], {"gy": along_y(i)})

    def share(all_ref, k, side):
        return remote(all_ref.at[:, core], all_ref.at[:, side], ss.at[k], rs.at[k], sibling)

    for p in range(2):
        for i in ORDER:
            first_a(p, i).start()
        loop(1, n_gx, lambda i: first_b(p, i).start())
    copies = [
        pltpu.make_async_copy(slab.at[:, gy, pl.ds(0, 8)], buf_a.at[0, gy], local.at[0]),
        pltpu.make_async_copy(slab.at[:, gy, pl.ds(8, 8)], buf_a.at[1, gy], local.at[1]),
        pltpu.make_async_copy(fx, fx_all.at[chip, core], local.at[2]),
        pltpu.make_async_copy(fy.at[core], fy_all.at[gy, core], local.at[3]),
        pltpu.make_async_copy(slab.at[gx, :, pl.ds(half, 8)], buf_b.at[0, gx], local.at[4]),
        pltpu.make_async_copy(slab.at[gx, :, pl.ds(half + 8, 8)], buf_b.at[1, gx], local.at[5]),
    ]
    for copy in copies:
        copy.start()
    mine_all = []
    for p in range(2):
        copies[p].wait()
        three(sa1.at[p], ra1.at[p]).wait_recv()
        loop(1, n_gx, lambda i: second_a(p, i).start())
        mine = pltpu.make_async_copy(buf_a.at[p, :, gx], plane.at[:, gx, pl.ds(8 * p, 8)], local.at[6 + p])
        mine.start()
        mine_all.append(mine)
        copies[4 + p].wait()
        fifteen(sb1.at[p], rb1.at[p]).wait_recv()
        for i in ORDER:
            second_b(p, i).start()
        mine = pltpu.make_async_copy(buf_b.at[p, :, gy], plane.at[gy, :, pl.ds(half + 8 * p, 8)], local.at[8 + p])
        mine.start()
        mine_all.append(mine)
    for i in ORDER:
        factor_y(i, gy).start()
    loop(1, n_gx // 2, lambda i: factor_x(i, chip).start())
    for p in range(2):
        fifteen(sa2.at[p], ra2.at[p]).wait_recv()
        three(sb2.at[p], rb2.at[p]).wait_recv()
    for mine in mine_all:
        mine.wait()

    for g in range(n_gy):
        p_high[g], p_low[g] = split(plane[g].reshape(512, 128))
    joined = lambda ref: jnp.concatenate([ref[g] for g in range(n_gy)], axis=1)

    def x_rows(q0, q1):
        parts = []
        for q in (q0, q1):
            rows = plane[:, :, pl.ds(pl.multiple_of(q * 8, 8), 8), :].reshape(n_gy, 128, 128)
            parts.append(jnp.concatenate([rows[g] for g in range(n_gy)], axis=1))
        rows = split(jnp.concatenate(parts, axis=0))
        return dot3(rows, (joined(p_high), joined(p_low)), ((1,), (1,)))

    def y_rows(q0, q1):
        rows = [jnp.concatenate([ref[q0], ref[q1]], axis=1) for ref in (p_high, p_low)]
        return dot3(rows, (joined(p_high), joined(p_low)), ((0,), (0,)))

    def x_part(i, slot):
        t = step(gy, i)
        return remote(total.at[t], got1.at[slot], s1.at[i], r1.at[slot], {"gy": t})

    def y_part(i, slot):
        t = step(x, i)
        return remote(total.at[t], got1.at[slot], s1.at[i], r1.at[slot], chip_at(t, y, gy))

    def swap(q):
        return remote(to_sib.at[q], got0.at[q], s0.at[q], r0.at[q], sibling)

    def grams(theirs, their_q, mine, my_q, part):
        for pair in ((2, 1), (3, 0)):
            value = theirs(step(their_q, pair[0]), step(their_q, pair[1]))
            for k, i in enumerate(pair):
                q = step(their_q, i)
                to_sib[q] = value[128 * k : 128 * k + 128]
                swap(q).start()
        for pair in ((2, 1), (3, 0)):
            value = mine(step(my_q, pair[0]), step(my_q, pair[1]))
            for k, i in enumerate(pair):
                q = step(my_q, i)
                swap(q).wait_recv()
                total[q] = value[128 * k : 128 * k + 128] + got0[q]
                if i:
                    part(i, my_q).start()

    @pl.when(core == 0)
    def _():
        grams(y_rows, x, x_rows, gy, x_part)

    @pl.when(core == 1)
    def _():
        grams(x_rows, gy, y_rows, x, y_part)

    copies[2].wait()
    copies[3].wait()
    for i in (1, 3, 2):
        factor_y(i, along_y(i)).wait()
    share(fy_all, 0, core).start()
    loop(1, n_gx // 2, lambda i: factor_x(i, lax.rem(chip + i, n_gx // 2)).wait())
    share(fx_all, 1, core).start()
    share(fy_all, 0, 1 - core).wait()
    whole = (joined(p_high), joined(p_low))
    inner = split(dot3(whole, split(fy_all[...].reshape(512, 256)), ((1,), (0,))))
    share(fx_all, 1, 1 - core).wait()
    product = dot3(split(fx_all[...].reshape(512, 256)), inner, ((0,), (0,)))
    product = product.reshape(n_gx, 2, 8, 256)
    upper, lower = product[:, 0].reshape(128, 256), product[:, 1].reshape(128, 256)
    lane = lax.broadcasted_iota(jnp.int32, (128, 128), 1)
    for g in range(n_gy):
        j = g // 2 * 128
        left, right = upper[:, j : j + 128], lower[:, j : j + 128]
        if g % 2 == 0:
            right = pltpu.roll(right, 64, 1)
        else:
            left = pltpu.roll(left, 64, 1)
        tiles[g] = jnp.where(lane < 64, left, right)

    def out1(i, slot):
        t = along_y(i)
        return remote(tiles.at[t], mid.at[slot], sc1.at[i], rc1.at[slot], {"gy": t})

    for i in ORDER:
        out1(i, gy).start()
    mine1 = pltpu.make_async_copy(tiles.at[gy], mid.at[gy], local.at[0])
    mine1.start()

    def x_piece(i, slot):
        j = lax.rem(x * 4 + y + i, 16)
        to_x, to_y = j // 4, lax.rem(j, 4)
        src = part1.at[(lax.rem(to_y, 2) * 4 + to_x) * 2 + to_y // 2]
        return remote(src, got2.at[slot], s2.at[i], r2.at[slot], chip_at(to_x, to_y, gy))

    def y_piece(i, slot):
        j = lax.rem(gy * 4 + y + i, 16)
        to_z, to_y = j // 4, lax.rem(j, 4)
        return remote(part1.at[j], got2.at[slot], s2.at[i], r2.at[slot], chip_at(x, to_y, to_z))

    def to_plane(i, slot):
        j = lax.rem(x * 4 + y + i, 16)
        dst = gram_y_t.at[slot]
        return remote(dst, dst, s4.at[i], r4.at[slot], chip_at(j // 4, lax.rem(j, 4), gy))

    def sum_parts(part, own):
        for i in (1, 3, 2):
            part(i, step(own, i)).wait()
        return (total[own] + got1[step(own, 2)]) + (got1[step(own, 1)] + got1[step(own, 3)])

    @pl.when(core == 0)
    def _():
        rows = sum_parts(x_part, gy).reshape(8, 2, 8, 512)
        even, odd = rows[:, 0].reshape(64, 512), rows[:, 1].reshape(64, 512)
        sub = lax.rem(lax.broadcasted_iota(jnp.int32, (64, 512), 0), 8)
        low = jnp.where(sub < 4, even, pltpu.roll(odd, 4, 0)).reshape(8, 8, 512)
        high = jnp.where(sub < 4, pltpu.roll(even, 60, 0), odd).reshape(8, 8, 512)
        by_tile = part1.reshape(8, 2, 4, 8, 128)
        for t in range(4):
            by_tile[:, 0, t] = low[:, :, 128 * t : 128 * t + 128]
            by_tile[:, 1, t] = high[:, :, 128 * t : 128 * t + 128]
        me = x * 4 + y
        loop(1, 16, lambda i: x_piece(i, me).start())

    @pl.when(core == 1)
    def _():
        rows = sum_parts(y_part, x)
        for z in range(4):
            part1[4 * z : 4 * z + 4] = rows[:, 128 * z : 128 * z + 128].reshape(4, 32, 128)
        me = gy * 4 + y
        loop(1, 16, lambda i: y_piece(i, me).start())

    mine1.wait()
    for i in (1, 3, 2):
        out1(i, along_y(i)).wait()
    mid4 = mid.reshape(n_gy, n_gx, 8, 128)

    def out2(i, owner):
        t = along_x(i)
        return remote(mid4.at[:, t], core_tiles.at[owner], sc2.at[i], rc2.at[owner], {"gx": t})

    loop(1, n_gx, lambda i: out2(i, gx).start())
    mine2 = pltpu.make_async_copy(mid4.at[:, gx], core_tiles.at[gx], local.at[1])
    mine2.start()

    to_sibling = remote(part2, last, s4.at[0], r4.at[16], sibling)
    all_rows = remote(gram_y_t, gram_y_t, s4.at[0], r4.at[17], sibling)

    @pl.when(core == 0)
    def _():
        me = x * 4 + y
        loop(1, 16, lambda i: x_piece(i, lax.rem(me + i, 16)).wait())
        got2[me] = part1[(y_lo * 4 + x) * 2 + sa]
        part2[...] = jnp.sum(got2[...], axis=0) * scale
        to_sibling.start()
        for t in range(4):
            gram_x[:, 128 * t : 128 * t + 128] = part2[8 * t : 8 * t + 4]
        to_sibling.wait_send()
        all_rows.wait_recv()

    @pl.when(core == 1)
    def _():
        me = gy * 4 + y
        loop(1, 16, lambda i: y_piece(i, lax.rem(me + i, 16)).wait())
        got2[me] = part1[me]
        here = x * 4 + y
        gram_y_t[here] = jnp.sum(got2[...], axis=0) * scale
        loop(1, 16, lambda i: to_plane(i, here).start())
        to_sibling.wait_recv()
        for t in range(4):
            gram_x[:, 128 * t : 128 * t + 128] = last[8 * t + 4 : 8 * t + 8]
        loop(1, 16, lambda i: to_plane(i, lax.rem(here + i, 16)).wait())
        all_rows.start()
        all_rows.wait_send()

    mine2.wait()
    loop(1, n_gx, lambda i: out2(i, along_x(i)).wait())
    loop(0, 4, lambda q: swap(q).wait_send())
    for p in range(2):
        three(sa1.at[p], ra1.at[p]).wait_send()
        fifteen(sb1.at[p], rb1.at[p]).wait_send()
        fifteen(sa2.at[p], ra2.at[p]).wait_send()
        three(sb2.at[p], rb2.at[p]).wait_send()


def finish_kernel(gx_in, gy_in, core_in, gx_out, gy_out, core_out):
    gx_out[...] = gx_in[...]
    gy_out[...] = gy_in[...].reshape(512, 128).T
    tile = core_in[...].reshape(64, 8, 128)
    core_out[:, 0:8, :] = tile[:, :, 0:64]
    core_out[:, 8:16, :] = tile[:, :, 64:128]


def shards(slab, factor_x, factor_y):
    z_cells, s_local, x_local, y_local = slab.shape
    n_gx, n_gy, n_sa = lax.axis_size("gx"), lax.axis_size("gy"), lax.axis_size("sa")
    scale = 1.0 / (y_local * n_gy * z_cells * s_local * n_sa)
    rank = factor_x.shape[1]
    vmem = pltpu.VMEM
    results = pl.pallas_call(
        functools.partial(tucker_kernel, scale),
        out_shape=(
            jax.ShapeDtypeStruct((4, 512), F32),
            jax.ShapeDtypeStruct((16, 32, 128), F32),
            jax.ShapeDtypeStruct((n_gx, n_gy, 8, 128), F32),
        ),
        in_specs=[HBM] * 3,
        out_specs=(VMEM,) * 3,
        scratch_shapes=[
            vmem((2, 4, 16, 8, 128), F32), vmem((2, 16, 4, 8, 128), F32), vmem((4, 16, 32, 128), F32),
            vmem((8, 2, 32, 256), F32), vmem((4, 2, 64, 256), F32),
            vmem((4, 512, 128), BF16), vmem((4, 512, 128), BF16),
            vmem((4, 128, 512), F32), vmem((4, 128, 512), F32), vmem((4, 128, 512), F32), vmem((4, 128, 512), F32),
            vmem((16, 32, 128), F32), vmem((16, 32, 128), F32), vmem((32, 128), F32), vmem((32, 128), F32),
            vmem((4, 128, 128), F32), vmem((4, 128, 128), F32),
            DMA((2,)), DMA((2,)), DMA((2,)), DMA((2,)), DMA((2,)), DMA((2,)), DMA((2,)), DMA((2,)),
            DMA((8,)), DMA((8,)), DMA((4,)), DMA((4,)), DMA((2,)), DMA((2,)),
            DMA((4,)), DMA((4,)), DMA((4,)), DMA((4,)), DMA((16,)), DMA((16,)), DMA((16,)), DMA((18,)),
            DMA((4,)), DMA((4,)), DMA((16,)), DMA((16,)), DMA((10,)),
        ],
        compiler_params=pltpu.CompilerParams(collective_id=0, has_side_effects=True, vmem_limit_bytes=56 << 20),
        name="tucker",
    )(
        slab.reshape(n_gx, n_gy, x_local, y_local), factor_x, factor_y.reshape(2, y_local // 2, rank)
    )
    gram_x, gram_y, core = pl.pallas_call(
        finish_kernel,
        out_shape=(
            jax.ShapeDtypeStruct((4, 512), F32),
            jax.ShapeDtypeStruct((128, 512), F32),
            jax.ShapeDtypeStruct((64, 16, 64), F32),
        ),
        in_specs=[VMEM] * 3,
        out_specs=(VMEM,) * 3,
        name="finish",
    )(*results)
    return gram_x, gram_y, core.reshape(z_cells, s_local, rank // n_gx, rank // n_gy)


def solution(mesh):
    in_specs = (P(None, "sa", "gx", "gy"), P("gx", None), P("gy", None))
    out_specs = (P(("gx", "gy", "sa"), None), P("gy", None), P(None, "sa", "gx", "gy"))
    return jax.shard_map(shards, mesh=mesh, in_specs=in_specs, out_specs=out_specs, check_vma=False)
```

```python
import functools

import jax
import jax.numpy as jnp
from jax import lax
from jax.experimental import pallas as pl
from jax.experimental.pallas import tpu as pltpu
from jax.sharding import PartitionSpec as P

MESH = pl.DeviceIdType.MESH
DMA = pltpu.SemaphoreType.DMA
F32 = jnp.float32
BF16 = jnp.bfloat16
VMEM = pl.BlockSpec(memory_space=pltpu.VMEM)
HBM = pl.BlockSpec(memory_space=pltpu.HBM)
ORDER = (2, 1, 3)


def loop(start, stop, body):
    def step(i, carry):
        body(i)
        return carry

    lax.fori_loop(start, stop, step, 0)


def remote(src, dst, send, recv, device):
    return pltpu.make_async_remote_copy(
        src_ref=src, dst_ref=dst, send_sem=send, recv_sem=recv, device_id=device, device_id_type=MESH
    )


def greet(devices_of, count):
    barrier = pltpu.get_barrier_semaphore()
    loop(1, count, lambda i: pl.semaphore_signal(barrier, 1, device_id=devices_of(i), device_id_type=MESH))


def split(value):
    high = value.astype(BF16)
    return high, (value - high.astype(F32)).astype(BF16)


def dot3(a, b, dims):
    (a_high, a_low), (b_high, b_low) = a, b
    dot = lambda p, q: lax.dot_general(p, q, (dims, ((), ())), preferred_element_type=F32)
    return dot(a_high, b_low) + dot(a_low, b_high) + dot(a_high, b_high)


def tucker_kernel(
    scale, slab, fx, fy, gram_x, gram_y_t, core_tiles,
    buf_a, buf_b, plane, fx_all, fy_all, p_high, p_low, to_sib, got0, total, got1, part1, got2, part2, last, tiles, mid,
    sa1, ra1, sa2, ra2, sb1, rb1, sb2, rb2, sfx, rfx, sfy, rfy, ss, rs,
    s0, r0, s1, r1, s2, r2, s4, r4, sc1, rc1, sc2, rc2, local,
):
    gx, gy, sa = lax.axis_index("gx"), lax.axis_index("gy"), lax.axis_index("sa")
    n_gx, n_gy = 16, 4
    chip, core = gx // 2, lax.rem(gx, 2)
    x, y_lo = lax.rem(chip, 4), chip // 4
    y = sa * 2 + y_lo
    half = 16
    step = lambda v, i: lax.rem(v + i, 4)
    along_x = lambda i: lax.rem(gx + i, n_gx)
    along_y = lambda i: lax.rem(gy + i, n_gy)
    sibling = {"gx": gx + 1 - 2 * core}

    def chip_at(to_x, to_y, to_z):
        return {"gx": lax.rem(to_y, 2) * 8 + to_x * 2 + core, "gy": to_z, "sa": to_y // 2}

    barrier = pltpu.get_barrier_semaphore()
    greet(lambda i: {"gx": along_x(i)}, n_gx)
    greet(lambda i: {"gy": along_y(i)}, n_gy)
    loop(0, 8, lambda i: pl.semaphore_signal(
        barrier, 1, device_id={"gx": i * 2 + core, "sa": 1 - sa}, device_id_type=MESH))

    @pl.when(core == 1)
    def _():
        for i in (1, 2, 3):
            for j in (1, 2, 3):
                pl.semaphore_signal(barrier, 1, device_id=chip_at(x, step(y, i), step(gy, j)), device_id_type=MESH)

    pl.semaphore_wait(barrier, n_gx + n_gy - 2 + 8 + 9 * core)

    def first_a(p, i):
        t = along_y(i)
        return remote(slab.at[:, t, pl.ds(8 * p, 8)], buf_a.at[p, gy], sa1.at[p], ra1.at[p], {"gy": t})

    def first_b(p, i):
        t = along_x(i)
        return remote(slab.at[t, :, pl.ds(half + 8 * p, 8)], buf_b.at[p, gx], sb1.at[p], rb1.at[p], {"gx": t})

    def second_a(p, i):
        t = along_x(i)
        dst = plane.at[:, gx, pl.ds(8 * p, 8)]
        return remote(buf_a.at[p, :, t], dst, sa2.at[p], ra2.at[p], {"gx": t})

    def second_b(p, i):
        t = along_y(i)
        dst = plane.at[gy, :, pl.ds(half + 8 * p, 8)]
        return remote(buf_b.at[p, :, t], dst, sb2.at[p], rb2.at[p], {"gy": t})

    def bytes_of(ref, send, recv):
        return remote(ref, ref, send, recv, sibling)

    three = lambda send, recv: bytes_of(buf_a.at[0, pl.ds(0, 3)], send, recv)
    fifteen = lambda send, recv: bytes_of(buf_b.at[0, pl.ds(0, 15)], send, recv)

    def factor_x(i, owner):
        t = lax.rem(chip + i, n_gx // 2)
        return remote(fx, fx_all.at[owner, core], sfx.at[i], rfx.at[owner], {"gx": t * 2 + core})

    def factor_y(i, owner):
        return remote(fy.at[core], fy_all.at[owner, core], sfy.at[i], rfy.at[owner], {"gy": along_y(i)})

    def share(all_ref, k, side):
        return remote(all_ref.at[:, core], all_ref.at[:, side], ss.at[k], rs.at[k], sibling)

    for p in range(2):
        for i in ORDER:
            first_a(p, i).start()
        loop(1, n_gx, lambda i: first_b(p, i).start())
    copies = [
        pltpu.make_async_copy(slab.at[:, gy, pl.ds(0, 8)], buf_a.at[0, gy], local.at[0]),
        pltpu.make_async_copy(slab.at[:, gy, pl.ds(8, 8)], buf_a.at[1, gy], local.at[1]),
        pltpu.make_async_copy(fx, fx_all.at[chip, core], local.at[2]),
        pltpu.make_async_copy(fy.at[core], fy_all.at[gy, core], local.at[3]),
        pltpu.make_async_copy(slab.at[gx, :, pl.ds(half, 8)], buf_b.at[0, gx], local.at[4]),
        pltpu.make_async_copy(slab.at[gx, :, pl.ds(half + 8, 8)], buf_b.at[1, gx], local.at[5]),
    ]
    for copy in copies:
        copy.start()
    mine_all = []
    for p in range(2):
        copies[p].wait()
        three(sa1.at[p], ra1.at[p]).wait_recv()
        loop(1, n_gx, lambda i: second_a(p, i).start())
        mine = pltpu.make_async_copy(buf_a.at[p, :, gx], plane.at[:, gx, pl.ds(8 * p, 8)], local.at[6 + p])
        mine.start()
        mine_all.append(mine)
        copies[4 + p].wait()
        fifteen(sb1.at[p], rb1.at[p]).wait_recv()
        for i in ORDER:
            second_b(p, i).start()
        mine = pltpu.make_async_copy(buf_b.at[p, :, gy], plane.at[gy, :, pl.ds(half + 8 * p, 8)], local.at[8 + p])
        mine.start()
        mine_all.append(mine)
    for i in ORDER:
        factor_y(i, gy).start()
    loop(1, n_gx // 2, lambda i: factor_x(i, chip).start())
    for p in range(2):
        fifteen(sa2.at[p], ra2.at[p]).wait_recv()
        three(sb2.at[p], rb2.at[p]).wait_recv()
    for mine in mine_all:
        mine.wait()

    for g in range(n_gy):
        p_high[g], p_low[g] = split(plane[g].reshape(512, 128))
    joined = lambda ref: jnp.concatenate([ref[g] for g in range(n_gy)], axis=1)

    def x_rows(q0, q1):
        parts = []
        for q in (q0, q1):
            rows = plane[:, :, pl.ds(pl.multiple_of(q * 8, 8), 8), :].reshape(n_gy, 128, 128)
            parts.append(jnp.concatenate([rows[g] for g in range(n_gy)], axis=1))
        rows = split(jnp.concatenate(parts, axis=0))
        return dot3(rows, (joined(p_high), joined(p_low)), ((1,), (1,)))

    def y_rows(q0, q1):
        rows = [jnp.concatenate([ref[q0], ref[q1]], axis=1) for ref in (p_high, p_low)]
        return dot3(rows, (joined(p_high), joined(p_low)), ((0,), (0,)))

    def x_part(i, slot):
        t = step(gy, i)
        return remote(total.at[t], got1.at[slot], s1.at[i], r1.at[slot], {"gy": t})

    def y_part(i, slot):
        t = step(x, i)
        return remote(total.at[t], got1.at[slot], s1.at[i], r1.at[slot], chip_at(t, y, gy))

    def swap(q):
        return remote(to_sib.at[q], got0.at[q], s0.at[q], r0.at[q], sibling)

    def grams(theirs, their_q, mine, my_q, part):
        for pair in ((2, 1), (3, 0)):
            value = theirs(step(their_q, pair[0]), step(their_q, pair[1]))
            for k, i in enumerate(pair):
                q = step(their_q, i)
                to_sib[q] = value[128 * k : 128 * k + 128]
                swap(q).start()
        for pair in ((2, 1), (3, 0)):
            value = mine(step(my_q, pair[0]), step(my_q, pair[1]))
            for k, i in enumerate(pair):
                q = step(my_q, i)
                swap(q).wait_recv()
                total[q] = value[128 * k : 128 * k + 128] + got0[q]
                if i:
                    part(i, my_q).start()

    @pl.when(core == 0)
    def _():
        grams(y_rows, x, x_rows, gy, x_part)

    @pl.when(core == 1)
    def _():
        grams(x_rows, gy, y_rows, x, y_part)

    copies[2].wait()
    copies[3].wait()
    for i in (1, 3, 2):
        factor_y(i, along_y(i)).wait()
    share(fy_all, 0, core).start()
    loop(1, n_gx // 2, lambda i: factor_x(i, lax.rem(chip + i, n_gx // 2)).wait())
    share(fx_all, 1, core).start()
    share(fy_all, 0, 1 - core).wait()
    whole = (joined(p_high), joined(p_low))
    inner = split(dot3(whole, split(fy_all[...].reshape(512, 256)), ((1,), (0,))))
    share(fx_all, 1, 1 - core).wait()
    product = dot3(split(fx_all[...].reshape(512, 256)), inner, ((0,), (0,)))
    product = product.reshape(n_gx, 2, 8, 256)
    upper, lower = product[:, 0].reshape(128, 256), product[:, 1].reshape(128, 256)
    lane = lax.broadcasted_iota(jnp.int32, (128, 128), 1)
    for g in range(n_gy):
        j = g // 2 * 128
        left, right = upper[:, j : j + 128], lower[:, j : j + 128]
        if g % 2 == 0:
            right = pltpu.roll(right, 64, 1)
        else:
            left = pltpu.roll(left, 64, 1)
        tiles[g] = jnp.where(lane < 64, left, right)

    def out1(i, slot):
        t = along_y(i)
        return remote(tiles.at[t], mid.at[slot], sc1.at[i], rc1.at[slot], {"gy": t})

    for i in ORDER:
        out1(i, gy).start()
    mine1 = pltpu.make_async_copy(tiles.at[gy], mid.at[gy], local.at[0])
    mine1.start()

    def x_piece(i, slot):
        j = lax.rem(x * 4 + y + i, 16)
        to_x, to_y = j // 4, lax.rem(j, 4)
        src = part1.at[(lax.rem(to_y, 2) * 4 + to_x) * 2 + to_y // 2]
        return remote(src, got2.at[slot], s2.at[i], r2.at[slot], chip_at(to_x, to_y, gy))

    def y_piece(i, slot):
        j = lax.rem(gy * 4 + y + i, 16)
        to_z, to_y = j // 4, lax.rem(j, 4)
        return remote(part1.at[j], got2.at[slot], s2.at[i], r2.at[slot], chip_at(x, to_y, to_z))

    def to_plane(i, slot):
        j = lax.rem(x * 4 + y + i, 16)
        dst = gram_y_t.at[slot]
        return remote(dst, dst, s4.at[i], r4.at[slot], chip_at(j // 4, lax.rem(j, 4), gy))

    def sum_parts(part, own):
        for i in (1, 3, 2):
            part(i, step(own, i)).wait()
        return (total[own] + got1[step(own, 2)]) + (got1[step(own, 1)] + got1[step(own, 3)])

    @pl.when(core == 0)
    def _():
        rows = sum_parts(x_part, gy).reshape(8, 2, 8, 512)
        even, odd = rows[:, 0].reshape(64, 512), rows[:, 1].reshape(64, 512)
        sub = lax.rem(lax.broadcasted_iota(jnp.int32, (64, 512), 0), 8)
        low = jnp.where(sub < 4, even, pltpu.roll(odd, 4, 0)).reshape(8, 8, 512)
        high = jnp.where(sub < 4, pltpu.roll(even, 60, 0), odd).reshape(8, 8, 512)
        by_tile = part1.reshape(8, 2, 4, 8, 128)
        for t in range(4):
            by_tile[:, 0, t] = low[:, :, 128 * t : 128 * t + 128]
            by_tile[:, 1, t] = high[:, :, 128 * t : 128 * t + 128]
        me = x * 4 + y
        loop(1, 16, lambda i: x_piece(i, me).start())

    @pl.when(core == 1)
    def _():
        rows = sum_parts(y_part, x)
        for z in range(4):
            part1[4 * z : 4 * z + 4] = rows[:, 128 * z : 128 * z + 128].reshape(4, 32, 128)
        me = gy * 4 + y
        loop(1, 16, lambda i: y_piece(i, me).start())

    mine1.wait()
    for i in (1, 3, 2):
        out1(i, along_y(i)).wait()
    mid4 = mid.reshape(n_gy, n_gx, 8, 128)

    def out2(i, owner):
        t = along_x(i)
        return remote(mid4.at[:, t], core_tiles.at[owner], sc2.at[i], rc2.at[owner], {"gx": t})

    loop(1, n_gx, lambda i: out2(i, gx).start())
    mine2 = pltpu.make_async_copy(mid4.at[:, gx], core_tiles.at[gx], local.at[1])
    mine2.start()

    to_sibling = remote(part2, last, s4.at[0], r4.at[16], sibling)
    all_rows = remote(gram_y_t, gram_y_t, s4.at[0], r4.at[17], sibling)

    def hand_over(j):
        return remote(gram_y_t.at[j], gram_y_t.at[j], s4.at[0], r4.at[17], sibling)


    @pl.when(core == 0)
    def _():
        me = x * 4 + y
        loop(1, 16, lambda i: x_piece(i, lax.rem(me + i, 16)).wait())
        got2[me] = part1[(y_lo * 4 + x) * 2 + sa]
        part2[...] = jnp.sum(got2[...], axis=0) * scale
        to_sibling.start()
        for t in range(4):
            gram_x[:, 128 * t : 128 * t + 128] = part2[8 * t : 8 * t + 4]
        to_sibling.wait_send()
        all_rows.wait_recv()

    @pl.when(core == 1)
    def _():
        me = gy * 4 + y
        loop(1, 16, lambda i: y_piece(i, lax.rem(me + i, 16)).wait())
        got2[me] = part1[me]
        here = x * 4 + y
        gram_y_t[here] = jnp.sum(got2[...], axis=0) * scale
        loop(1, 16, lambda i: to_plane(i, here).start())
        to_sibling.wait_recv()
        for t in range(4):
            gram_x[:, 128 * t : 128 * t + 128] = last[8 * t + 4 : 8 * t + 8]
        hand_over(here).start()
        for i in (12, 4, 3, 1, 15, 11, 13, 5, 7, 9, 8, 2, 14, 6, 10):
            j = lax.rem(here + i, 16)
            to_plane(i, j).wait_recv()
            hand_over(j).start()
        loop(1, 16, lambda i: to_plane(i, here).wait_send())
        all_rows.wait_send()

    mine2.wait()
    loop(1, n_gx, lambda i: out2(i, along_x(i)).wait())
    loop(0, 4, lambda q: swap(q).wait_send())
    for p in range(2):
        three(sa1.at[p], ra1.at[p]).wait_send()
        fifteen(sb1.at[p], rb1.at[p]).wait_send()
        fifteen(sa2.at[p], ra2.at[p]).wait_send()
        three(sb2.at[p], rb2.at[p]).wait_send()


def finish_kernel(gx_in, gy_in, core_in, gx_out, gy_out, core_out):
    gx_out[...] = gx_in[...]
    gy_out[...] = gy_in[...].reshape(512, 128).T
    tile = core_in[...].reshape(64, 8, 128)
    core_out[:, 0:8, :] = tile[:, :, 0:64]
    core_out[:, 8:16, :] = tile[:, :, 64:128]


def shards(slab, factor_x, factor_y):
    z_cells, s_local, x_local, y_local = slab.shape
    n_gx, n_gy, n_sa = lax.axis_size("gx"), lax.axis_size("gy"), lax.axis_size("sa")
    scale = 1.0 / (y_local * n_gy * z_cells * s_local * n_sa)
    rank = factor_x.shape[1]
    vmem = pltpu.VMEM
    results = pl.pallas_call(
        functools.partial(tucker_kernel, scale),
        out_shape=(
            jax.ShapeDtypeStruct((4, 512), F32),
            jax.ShapeDtypeStruct((16, 32, 128), F32),
            jax.ShapeDtypeStruct((n_gx, n_gy, 8, 128), F32),
        ),
        in_specs=[HBM] * 3,
        out_specs=(VMEM,) * 3,
        scratch_shapes=[
            vmem((2, 4, 16, 8, 128), F32), vmem((2, 16, 4, 8, 128), F32), vmem((4, 16, 32, 128), F32),
            vmem((8, 2, 32, 256), F32), vmem((4, 2, 64, 256), F32),
            vmem((4, 512, 128), BF16), vmem((4, 512, 128), BF16),
            vmem((4, 128, 512), F32), vmem((4, 128, 512), F32), vmem((4, 128, 512), F32), vmem((4, 128, 512), F32),
            vmem((16, 32, 128), F32), vmem((16, 32, 128), F32), vmem((32, 128), F32), vmem((32, 128), F32),
            vmem((4, 128, 128), F32), vmem((4, 128, 128), F32),
            DMA((2,)), DMA((2,)), DMA((2,)), DMA((2,)), DMA((2,)), DMA((2,)), DMA((2,)), DMA((2,)),
            DMA((8,)), DMA((8,)), DMA((4,)), DMA((4,)), DMA((2,)), DMA((2,)),
            DMA((4,)), DMA((4,)), DMA((4,)), DMA((4,)), DMA((16,)), DMA((16,)), DMA((16,)), DMA((18,)),
            DMA((4,)), DMA((4,)), DMA((16,)), DMA((16,)), DMA((10,)),
        ],
        compiler_params=pltpu.CompilerParams(collective_id=0, has_side_effects=True, vmem_limit_bytes=40 << 20),
        name="tucker",
    )(
        *(pltpu.with_memory_space_constraint(v, pltpu.HBM) for v in (
            slab.reshape(n_gx, n_gy, x_local, y_local), factor_x, factor_y.reshape(2, y_local // 2, rank)))
    )
    gram_x, gram_y, core = pl.pallas_call(
        finish_kernel,
        out_shape=(
            jax.ShapeDtypeStruct((4, 512), F32),
            jax.ShapeDtypeStruct((128, 512), F32),
            jax.ShapeDtypeStruct((64, 16, 64), F32),
        ),
        in_specs=[VMEM] * 3,
        out_specs=(VMEM,) * 3,
        compiler_params=pltpu.CompilerParams(vmem_limit_bytes=40 << 20),
        name="finish",
    )(*results)
    return gram_x, gram_y, core.reshape(z_cells, s_local, rank // n_gx, rank // n_gy)


def solution(mesh):
    in_specs = (P(None, "sa", "gx", "gy"), P("gx", None), P("gy", None))
    out_specs = (P(("gx", "gy", "sa"), None), P("gy", None), P(None, "sa", "gx", "gy"))
    return jax.shard_map(shards, mesh=mesh, in_specs=in_specs, out_specs=out_specs, check_vma=False)
```

```python
import functools

import jax
import jax.numpy as jnp
from jax import lax
from jax.experimental import pallas as pl
from jax.experimental.pallas import tpu as pltpu
from jax.sharding import PartitionSpec as P

MESH = pl.DeviceIdType.MESH
DMA = pltpu.SemaphoreType.DMA
F32 = jnp.float32
BF16 = jnp.bfloat16
VMEM = pl.BlockSpec(memory_space=pltpu.VMEM)
HBM = pl.BlockSpec(memory_space=pltpu.HBM)
ORDER = (2, 1, 3)


def loop(start, stop, body):
    def step(i, carry):
        body(i)
        return carry

    lax.fori_loop(start, stop, step, 0)


def remote(src, dst, send, recv, device):
    return pltpu.make_async_remote_copy(
        src_ref=src, dst_ref=dst, send_sem=send, recv_sem=recv, device_id=device, device_id_type=MESH
    )


def greet(devices_of, count):
    barrier = pltpu.get_barrier_semaphore()
    loop(1, count, lambda i: pl.semaphore_signal(barrier, 1, device_id=devices_of(i), device_id_type=MESH))


def split(value):
    high = value.astype(BF16)
    return high, (value - high.astype(F32)).astype(BF16)


def dot3(a, b, dims):
    (a_high, a_low), (b_high, b_low) = a, b
    dot = lambda p, q: lax.dot_general(p, q, (dims, ((), ())), preferred_element_type=F32)
    return dot(a_high, b_low) + dot(a_low, b_high) + dot(a_high, b_high)


def tucker_kernel(
    scale, slab, fx, fy, gram_x, gram_y_t, core_tiles,
    buf_a, buf_b, plane, fx_all, fy_all, p_high, p_low, to_sib, got0, total, got1, part1, got2, part2, last, tiles, mid,
    sa1, ra1, sa2, ra2, sb1, rb1, sb2, rb2, sfx, rfx, sfy, rfy, ss, rs,
    s0, r0, s1, r1, s2, r2, s4, r4, sc1, rc1, sc2, rc2, local,
):
    gx, gy, sa = lax.axis_index("gx"), lax.axis_index("gy"), lax.axis_index("sa")
    n_gx, n_gy = 16, 4
    chip, core = gx // 2, lax.rem(gx, 2)
    x, y_lo = lax.rem(chip, 4), chip // 4
    y = sa * 2 + y_lo
    half = 16
    step = lambda v, i: lax.rem(v + i, 4)
    along_x = lambda i: lax.rem(gx + i, n_gx)
    along_y = lambda i: lax.rem(gy + i, n_gy)
    sibling = {"gx": gx + 1 - 2 * core}

    def chip_at(to_x, to_y, to_z):
        return {"gx": lax.rem(to_y, 2) * 8 + to_x * 2 + core, "gy": to_z, "sa": to_y // 2}

    barrier = pltpu.get_barrier_semaphore()
    greet(lambda i: {"gx": along_x(i)}, n_gx)
    greet(lambda i: {"gy": along_y(i)}, n_gy)
    loop(0, 8, lambda i: pl.semaphore_signal(
        barrier, 1, device_id={"gx": i * 2 + core, "sa": 1 - sa}, device_id_type=MESH))

    @pl.when(core == 1)
    def _():
        for i in (1, 2, 3):
            for j in (1, 2, 3):
                pl.semaphore_signal(barrier, 1, device_id=chip_at(x, step(y, i), step(gy, j)), device_id_type=MESH)

    pl.semaphore_wait(barrier, n_gx + n_gy - 2 + 8 + 9 * core)

    def first_a(p, i):
        t = along_y(i)
        return remote(slab.at[:, t, pl.ds(8 * p, 8)], buf_a.at[p, gy], sa1.at[p], ra1.at[p], {"gy": t})

    def first_b(p, i):
        t = along_x(i)
        return remote(slab.at[t, :, pl.ds(half + 8 * p, 8)], buf_b.at[p, gx], sb1.at[p], rb1.at[p], {"gx": t})

    def second_a(p, i):
        t = along_x(i)
        dst = plane.at[:, gx, pl.ds(8 * p, 8)]
        return remote(buf_a.at[p, :, t], dst, sa2.at[p], ra2.at[p], {"gx": t})

    def second_b(p, i):
        t = along_y(i)
        dst = plane.at[gy, :, pl.ds(half + 8 * p, 8)]
        return remote(buf_b.at[p, :, t], dst, sb2.at[p], rb2.at[p], {"gy": t})

    def bytes_of(ref, send, recv):
        return remote(ref, ref, send, recv, sibling)

    three = lambda send, recv: bytes_of(buf_a.at[0, pl.ds(0, 3)], send, recv)
    fifteen = lambda send, recv: bytes_of(buf_b.at[0, pl.ds(0, 15)], send, recv)

    def factor_x(i, owner):
        t = lax.rem(chip + i, n_gx // 2)
        return remote(fx, fx_all.at[owner, core], sfx.at[i], rfx.at[owner], {"gx": t * 2 + core})

    def factor_y(i, owner):
        return remote(fy.at[core], fy_all.at[owner, core], sfy.at[i], rfy.at[owner], {"gy": along_y(i)})

    def share(all_ref, k, side):
        return remote(all_ref.at[:, core], all_ref.at[:, side], ss.at[k], rs.at[k], sibling)

    for p in range(2):
        for i in ORDER:
            first_a(p, i).start()
        loop(1, n_gx, lambda i: first_b(p, i).start())
    copies = [
        pltpu.make_async_copy(slab.at[:, gy, pl.ds(0, 8)], buf_a.at[0, gy], local.at[0]),
        pltpu.make_async_copy(slab.at[:, gy, pl.ds(8, 8)], buf_a.at[1, gy], local.at[1]),
        pltpu.make_async_copy(fx, fx_all.at[chip, core], local.at[2]),
        pltpu.make_async_copy(fy.at[core], fy_all.at[gy, core], local.at[3]),
        pltpu.make_async_copy(slab.at[gx, :, pl.ds(half, 8)], buf_b.at[0, gx], local.at[4]),
        pltpu.make_async_copy(slab.at[gx, :, pl.ds(half + 8, 8)], buf_b.at[1, gx], local.at[5]),
    ]
    for copy in copies:
        copy.start()
    mine_all = []
    for p in range(2):
        copies[p].wait()
        three(sa1.at[p], ra1.at[p]).wait_recv()
        loop(1, n_gx, lambda i: second_a(p, i).start())
        mine = pltpu.make_async_copy(buf_a.at[p, :, gx], plane.at[:, gx, pl.ds(8 * p, 8)], local.at[6 + p])
        mine.start()
        mine_all.append(mine)
        copies[4 + p].wait()
        fifteen(sb1.at[p], rb1.at[p]).wait_recv()
        for i in ORDER:
            second_b(p, i).start()
        mine = pltpu.make_async_copy(buf_b.at[p, :, gy], plane.at[gy, :, pl.ds(half + 8 * p, 8)], local.at[8 + p])
        mine.start()
        mine_all.append(mine)
    for i in ORDER:
        factor_y(i, gy).start()
    loop(1, n_gx // 2, lambda i: factor_x(i, chip).start())
    for p in range(2):
        fifteen(sa2.at[p], ra2.at[p]).wait_recv()
        three(sb2.at[p], rb2.at[p]).wait_recv()
    for mine in mine_all:
        mine.wait()

    for g in range(n_gy):
        p_high[g], p_low[g] = split(plane[g].reshape(512, 128))
    joined = lambda ref: jnp.concatenate([ref[g] for g in range(n_gy)], axis=1)

    def x_rows(q0, q1):
        parts = []
        for q in (q0, q1):
            rows = plane[:, :, pl.ds(pl.multiple_of(q * 8, 8), 8), :].reshape(n_gy, 128, 128)
            parts.append(jnp.concatenate([rows[g] for g in range(n_gy)], axis=1))
        rows = split(jnp.concatenate(parts, axis=0))
        return dot3(rows, (joined(p_high), joined(p_low)), ((1,), (1,)))

    def y_rows(q0, q1):
        rows = [jnp.concatenate([ref[q0], ref[q1]], axis=1) for ref in (p_high, p_low)]
        return dot3(rows, (joined(p_high), joined(p_low)), ((0,), (0,)))

    def x_part(i, slot, h):
        t = step(gy, i)
        return remote(total.at[t, h], got1.at[slot, h], s1.at[i, h], r1.at[slot, h], {"gy": t})

    def y_part(i, slot, h):
        t = step(x, i)
        return remote(total.at[t, h], got1.at[slot, h], s1.at[i, h], r1.at[slot, h], chip_at(t, y, gy))

    def x_half(rows, h):
        columns = rows[:, 256 * h : 256 * h + 256]
        return jnp.concatenate([columns[0:64], columns[64:128]], axis=1)

    def y_half(rows, h):
        return rows.reshape(4, 2, 16, 512)[:, h].reshape(64, 512)

    def swap(q):
        return remote(to_sib.at[q], got0.at[q], s0.at[q], r0.at[q], sibling)

    def grams(theirs, their_q, mine, my_q, part, half_of):
        for pair in ((2, 1), (3, 0)):
            value = theirs(step(their_q, pair[0]), step(their_q, pair[1]))
            for k, i in enumerate(pair):
                q = step(their_q, i)
                to_sib[q] = value[128 * k : 128 * k + 128]
                swap(q).start()
        def own(pair):
            value = mine(step(my_q, pair[0]), step(my_q, pair[1]))
            for k, i in enumerate(pair):
                q = step(my_q, i)
                swap(q).wait_recv()
                rows = value[128 * k : 128 * k + 128] + got0[q]
                for h in range(2):
                    total[q, h] = half_of(rows, h)

        own((2, 1))
        part(2, my_q, 0).start()
        part(1, my_q, 0).start()
        own((3, 0))
        for i, h in ((3, 0), (2, 1), (1, 1), (3, 1)):
            part(i, my_q, h).start()

    @pl.when(core == 0)
    def _():
        grams(y_rows, x, x_rows, gy, x_part, x_half)

    @pl.when(core == 1)
    def _():
        grams(x_rows, gy, y_rows, x, y_part, y_half)

    copies[2].wait()
    copies[3].wait()
    for i in (1, 3, 2):
        factor_y(i, along_y(i)).wait()
    share(fy_all, 0, core).start()
    loop(1, n_gx // 2, lambda i: factor_x(i, lax.rem(chip + i, n_gx // 2)).wait())
    share(fx_all, 1, core).start()
    share(fy_all, 0, 1 - core).wait()
    whole = (joined(p_high), joined(p_low))
    inner = split(dot3(whole, split(fy_all[...].reshape(512, 256)), ((1,), (0,))))
    share(fx_all, 1, 1 - core).wait()
    product = dot3(split(fx_all[...].reshape(512, 256)), inner, ((0,), (0,)))
    product = product.reshape(n_gx, 2, 8, 256)
    upper, lower = product[:, 0].reshape(128, 256), product[:, 1].reshape(128, 256)
    lane = lax.broadcasted_iota(jnp.int32, (128, 128), 1)
    for g in range(n_gy):
        j = g // 2 * 128
        left, right = upper[:, j : j + 128], lower[:, j : j + 128]
        if g % 2 == 0:
            right = pltpu.roll(right, 64, 1)
        else:
            left = pltpu.roll(left, 64, 1)
        tiles[g] = jnp.where(lane < 64, left, right)

    def out1(i, slot):
        t = along_y(i)
        return remote(tiles.at[t], mid.at[slot], sc1.at[i], rc1.at[slot], {"gy": t})

    for i in ORDER:
        out1(i, gy).start()
    mine1 = pltpu.make_async_copy(tiles.at[gy], mid.at[gy], local.at[0])
    mine1.start()

    def x_piece(i, slot, h):
        j = lax.rem(x * 4 + y + i, 16)
        to_x, to_y = j // 4, lax.rem(j, 4)
        src = part1.at[h, (lax.rem(to_y, 2) * 4 + to_x) * 2 + to_y // 2]
        return remote(src, got2.at[h, slot], s2.at[h], r2.at[h], chip_at(to_x, to_y, gy))

    def y_piece(i, slot, h):
        j = lax.rem(gy * 4 + y + i, 16)
        to_z, to_y = j // 4, lax.rem(j, 4)
        return remote(part1.at[h, j], got2.at[h, slot], s2.at[h], r2.at[h], chip_at(x, to_y, to_z))

    def pieces(h):
        return bytes_of(got2.at[h, pl.ds(0, 15)], s2.at[h], r2.at[h])

    def to_plane(i, slot):
        j = lax.rem(x * 4 + y + i, 16)
        dst = gram_y_t.at[slot]
        return remote(dst, dst, s4.at[i], r4.at[slot], chip_at(j // 4, lax.rem(j, 4), gy))

    def sum_parts(part, own, h):
        for i in (1, 3, 2):
            part(i, step(own, i), h).wait()
        return (total[own, h] + got1[step(own, 2), h]) + (got1[step(own, 1), h] + got1[step(own, 3), h])

    @pl.when(core == 0)
    def _():
        for h in range(2):
            rows = sum_parts(x_part, gy, h)
            rows = jnp.concatenate([rows[:, 0:256], rows[:, 256:512]], axis=0).reshape(8, 2, 8, 256)
            even, odd = rows[:, 0].reshape(64, 256), rows[:, 1].reshape(64, 256)
            sub = lax.rem(lax.broadcasted_iota(jnp.int32, (64, 256), 0), 8)
            low = jnp.where(sub < 4, even, pltpu.roll(odd, 4, 0)).reshape(8, 8, 256)
            high = jnp.where(sub < 4, pltpu.roll(even, 60, 0), odd).reshape(8, 8, 256)
            by_tile = part1.reshape(2, 8, 2, 2, 8, 128)
            for t in range(2):
                by_tile[h, :, 0, t] = low[:, :, 128 * t : 128 * t + 128]
                by_tile[h, :, 1, t] = high[:, :, 128 * t : 128 * t + 128]
            me = x * 4 + y
            loop(1, 16, lambda i: x_piece(i, me, h).start())

    @pl.when(core == 1)
    def _():
        for h in range(2):
            rows = sum_parts(y_part, x, h)
            for z in range(4):
                part1[h, 4 * z : 4 * z + 4] = rows[:, 128 * z : 128 * z + 128].reshape(4, 16, 128)
            me = gy * 4 + y
            loop(1, 16, lambda i: y_piece(i, me, h).start())

    mine1.wait()
    for i in (1, 3, 2):
        out1(i, along_y(i)).wait()
    mid4 = mid.reshape(n_gy, n_gx, 8, 128)

    def out2(i, owner):
        t = along_x(i)
        return remote(mid4.at[:, t], core_tiles.at[owner], sc2.at[i], rc2.at[owner], {"gx": t})

    loop(1, n_gx, lambda i: out2(i, gx).start())
    mine2 = pltpu.make_async_copy(mid4.at[:, gx], core_tiles.at[gx], local.at[1])
    mine2.start()

    to_sibling = remote(part2, last, s4.at[0], r4.at[16], sibling)
    all_rows = remote(gram_y_t, gram_y_t, s4.at[0], r4.at[17], sibling)

    def hand_over(j):
        return remote(gram_y_t.at[j], gram_y_t.at[j], s4.at[0], r4.at[17], sibling)


    @pl.when(core == 0)
    def _():
        me = x * 4 + y
        for h in range(2):
            pieces(h).wait()
            got2[h, me] = part1[h, (y_lo * 4 + x) * 2 + sa]
            part2[16 * h : 16 * h + 16] = jnp.sum(got2[h], axis=0) * scale
        to_sibling.start()
        for t in range(4):
            gram_x[:, 128 * t : 128 * t + 128] = part2[8 * t : 8 * t + 4]
        to_sibling.wait_send()
        all_rows.wait_recv()

    @pl.when(core == 1)
    def _():
        me = gy * 4 + y
        here = x * 4 + y
        for h in range(2):
            pieces(h).wait()
            got2[h, me] = part1[h, me]
            gram_y_t[here, 16 * h : 16 * h + 16] = jnp.sum(got2[h], axis=0) * scale
        loop(1, 16, lambda i: to_plane(i, here).start())
        to_sibling.wait_recv()
        for t in range(4):
            gram_x[:, 128 * t : 128 * t + 128] = last[8 * t + 4 : 8 * t + 8]
        hand_over(here).start()
        for i in (12, 4, 3, 1, 15, 11, 13, 5, 7, 9, 8, 2, 14, 6, 10):
            j = lax.rem(here + i, 16)
            to_plane(i, j).wait_recv()
            hand_over(j).start()
        loop(1, 16, lambda i: to_plane(i, here).wait_send())
        all_rows.wait_send()

    mine2.wait()
    loop(1, n_gx, lambda i: out2(i, along_x(i)).wait())
    loop(0, 4, lambda q: swap(q).wait_send())
    for p in range(2):
        three(sa1.at[p], ra1.at[p]).wait_send()
        fifteen(sb1.at[p], rb1.at[p]).wait_send()
        fifteen(sa2.at[p], ra2.at[p]).wait_send()
        three(sb2.at[p], rb2.at[p]).wait_send()


def finish_kernel(gx_in, gy_in, core_in, gx_out, gy_out, core_out):
    gx_out[...] = gx_in[...]
    gy_out[...] = gy_in[...].reshape(512, 128).T
    tile = core_in[...].reshape(64, 8, 128)
    core_out[:, 0:8, :] = tile[:, :, 0:64]
    core_out[:, 8:16, :] = tile[:, :, 64:128]


def shards(slab, factor_x, factor_y):
    z_cells, s_local, x_local, y_local = slab.shape
    n_gx, n_gy, n_sa = lax.axis_size("gx"), lax.axis_size("gy"), lax.axis_size("sa")
    scale = 1.0 / (y_local * n_gy * z_cells * s_local * n_sa)
    rank = factor_x.shape[1]
    vmem = pltpu.VMEM
    results = pl.pallas_call(
        functools.partial(tucker_kernel, scale),
        out_shape=(
            jax.ShapeDtypeStruct((4, 512), F32),
            jax.ShapeDtypeStruct((16, 32, 128), F32),
            jax.ShapeDtypeStruct((n_gx, n_gy, 8, 128), F32),
        ),
        in_specs=[HBM] * 3,
        out_specs=(VMEM,) * 3,
        scratch_shapes=[
            vmem((2, 4, 16, 8, 128), F32), vmem((2, 16, 4, 8, 128), F32), vmem((4, 16, 32, 128), F32),
            vmem((8, 2, 32, 256), F32), vmem((4, 2, 64, 256), F32),
            vmem((4, 512, 128), BF16), vmem((4, 512, 128), BF16),
            vmem((4, 128, 512), F32), vmem((4, 128, 512), F32), vmem((4, 2, 64, 512), F32), vmem((4, 2, 64, 512), F32),
            vmem((2, 16, 16, 128), F32), vmem((2, 16, 16, 128), F32), vmem((32, 128), F32), vmem((32, 128), F32),
            vmem((4, 128, 128), F32), vmem((4, 128, 128), F32),
            DMA((2,)), DMA((2,)), DMA((2,)), DMA((2,)), DMA((2,)), DMA((2,)), DMA((2,)), DMA((2,)),
            DMA((8,)), DMA((8,)), DMA((4,)), DMA((4,)), DMA((2,)), DMA((2,)),
            DMA((4,)), DMA((4,)), DMA((4, 2)), DMA((4, 2)), DMA((2,)), DMA((2,)), DMA((16,)), DMA((18,)),
            DMA((4,)), DMA((4,)), DMA((16,)), DMA((16,)), DMA((10,)),
        ],
        compiler_params=pltpu.CompilerParams(collective_id=0, has_side_effects=True, vmem_limit_bytes=40 << 20),
        name="tucker",
    )(
        *(pltpu.with_memory_space_constraint(v, pltpu.HBM) for v in (
            slab.reshape(n_gx, n_gy, x_local, y_local), factor_x, factor_y.reshape(2, y_local // 2, rank)))
    )
    gram_x, gram_y, core = pl.pallas_call(
        finish_kernel,
        out_shape=(
            jax.ShapeDtypeStruct((4, 512), F32),
            jax.ShapeDtypeStruct((128, 512), F32),
            jax.ShapeDtypeStruct((64, 16, 64), F32),
        ),
        in_specs=[VMEM] * 3,
        out_specs=(VMEM,) * 3,
        compiler_params=pltpu.CompilerParams(vmem_limit_bytes=40 << 20),
        name="finish",
    )(*results)
    return gram_x, gram_y, core.reshape(z_cells, s_local, rank // n_gx, rank // n_gy)


def solution(mesh):
    in_specs = (P(None, "sa", "gx", "gy"), P("gx", None), P("gy", None))
    out_specs = (P(("gx", "gy", "sa"), None), P("gy", None), P(None, "sa", "gx", "gy"))
    return jax.shard_map(shards, mesh=mesh, in_specs=in_specs, out_specs=out_specs, check_vma=False)
```

```python
import functools

import jax
import jax.numpy as jnp
from jax import lax
from jax.experimental import pallas as pl
from jax.experimental.pallas import tpu as pltpu
from jax.sharding import PartitionSpec as P

MESH = pl.DeviceIdType.MESH
DMA = pltpu.SemaphoreType.DMA
F32 = jnp.float32
BF16 = jnp.bfloat16
VMEM = pl.BlockSpec(memory_space=pltpu.VMEM)
HBM = pl.BlockSpec(memory_space=pltpu.HBM)
ORDER = (2, 1, 3)
FAR_PAIRS = (
    (2, 2), (2, 1), (1, 2), (2, 3), (3, 2), (1, 1), (3, 3), (1, 3), (3, 1), (2, 0), (0, 2), (1, 0), (0, 1), (3, 0), (0, 3),
)
FAR_FIRST = (
    (2, 1, 0), (2, 1, 1), (1, 1, 0), (3, 1, 1), (2, 0, 0), (0, 1, 0), (1, 1, 1), (3, 1, 0),
    (2, 0, 1), (0, 1, 1), (1, 0, 0), (3, 0, 0), (1, 0, 1), (3, 0, 1), (0, 0, 1),
)


def loop(start, stop, body):
    def step(i, carry):
        body(i)
        return carry

    lax.fori_loop(start, stop, step, 0)


def remote(src, dst, send, recv, device):
    return pltpu.make_async_remote_copy(
        src_ref=src, dst_ref=dst, send_sem=send, recv_sem=recv, device_id=device, device_id_type=MESH
    )


def greet(devices_of, count):
    barrier = pltpu.get_barrier_semaphore()
    loop(1, count, lambda i: pl.semaphore_signal(barrier, 1, device_id=devices_of(i), device_id_type=MESH))


def split(value):
    high = value.astype(BF16)
    return high, (value - high.astype(F32)).astype(BF16)


def dot3(a, b, dims):
    (a_high, a_low), (b_high, b_low) = a, b
    dot = lambda p, q: lax.dot_general(p, q, (dims, ((), ())), preferred_element_type=F32)
    return dot(a_high, b_low) + dot(a_low, b_high) + dot(a_high, b_high)


def tucker_kernel(
    scale, slab, fx, fy, gram_x, gram_y_t, core_tiles,
    buf_a, buf_b, plane, fx_all, fy_all, p_high, p_low, to_sib, got0, total, got1, part1, got2, part2, last, tiles, mid,
    sa1, ra1, sa2, ra2, sb1, rb1, sb2, rb2, sfx, rfx, sfy, rfy, ss, rs,
    s0, r0, s1, r1, s2, r2, s4, r4, sc1, rc1, sc2, rc2, local,
):
    gx, gy, sa = lax.axis_index("gx"), lax.axis_index("gy"), lax.axis_index("sa")
    n_gx, n_gy = 16, 4
    chip, core = gx // 2, lax.rem(gx, 2)
    x, y_lo = lax.rem(chip, 4), chip // 4
    y = sa * 2 + y_lo
    half = 16
    step = lambda v, i: lax.rem(v + i, 4)
    along_x = lambda i: lax.rem(gx + i, n_gx)
    along_y = lambda i: lax.rem(gy + i, n_gy)
    sibling = {"gx": gx + 1 - 2 * core}

    def chip_at(to_x, to_y, to_z):
        return {"gx": lax.rem(to_y, 2) * 8 + to_x * 2 + core, "gy": to_z, "sa": to_y // 2}

    barrier = pltpu.get_barrier_semaphore()
    greet(lambda i: {"gx": along_x(i)}, n_gx)
    greet(lambda i: {"gy": along_y(i)}, n_gy)
    loop(0, 8, lambda i: pl.semaphore_signal(
        barrier, 1, device_id={"gx": i * 2 + core, "sa": 1 - sa}, device_id_type=MESH))

    @pl.when(core == 1)
    def _():
        for i in (1, 2, 3):
            for j in (1, 2, 3):
                pl.semaphore_signal(barrier, 1, device_id=chip_at(x, step(y, i), step(gy, j)), device_id_type=MESH)

    pl.semaphore_wait(barrier, n_gx + n_gy - 2 + 8 + 9 * core)

    def near(steps):
        dx, dy, dc = steps
        return lax.rem(y_lo + dy, 2) * 8 + step(x, dx) * 2 + lax.rem(core + dc, 2)

    def first_a(p, i):
        t = along_y(i)
        return remote(slab.at[:, t, pl.ds(8 * p, 8)], buf_a.at[p, gy], sa1.at[p], ra1.at[p], {"gy": t})

    def first_b(p, steps):
        t = near(steps)
        return remote(slab.at[t, :, pl.ds(half + 8 * p, 8)], buf_b.at[p, gx], sb1.at[p], rb1.at[p], {"gx": t})

    def second_a(p, steps):
        t = near(steps)
        dst = plane.at[:, gx, pl.ds(8 * p, 8)]
        return remote(buf_a.at[p, :, t], dst, sa2.at[p], ra2.at[p], {"gx": t})

    def second_b(p, i):
        t = along_y(i)
        dst = plane.at[gy, :, pl.ds(half + 8 * p, 8)]
        return remote(buf_b.at[p, :, t], dst, sb2.at[p], rb2.at[p], {"gy": t})

    def bytes_of(ref, send, recv):
        return remote(ref, ref, send, recv, sibling)

    three = lambda send, recv: bytes_of(buf_a.at[0, pl.ds(0, 3)], send, recv)
    fifteen = lambda send, recv: bytes_of(buf_b.at[0, pl.ds(0, 15)], send, recv)

    def factor_x(i, owner):
        t = lax.rem(chip + i, n_gx // 2)
        return remote(fx, fx_all.at[owner, core], sfx.at[i], rfx.at[owner], {"gx": t * 2 + core})

    def factor_y(i, owner):
        return remote(fy.at[core], fy_all.at[owner, core], sfy.at[i], rfy.at[owner], {"gy": along_y(i)})

    def share(all_ref, k, side):
        return remote(all_ref.at[:, core], all_ref.at[:, side], ss.at[k], rs.at[k], sibling)

    for p in range(2):
        for i in ORDER:
            first_a(p, i).start()
        for steps in FAR_FIRST:
            first_b(p, steps).start()
    copies = [
        pltpu.make_async_copy(slab.at[:, gy, pl.ds(0, 8)], buf_a.at[0, gy], local.at[0]),
        pltpu.make_async_copy(slab.at[:, gy, pl.ds(8, 8)], buf_a.at[1, gy], local.at[1]),
        pltpu.make_async_copy(fx, fx_all.at[chip, core], local.at[2]),
        pltpu.make_async_copy(fy.at[core], fy_all.at[gy, core], local.at[3]),
        pltpu.make_async_copy(slab.at[gx, :, pl.ds(half, 8)], buf_b.at[0, gx], local.at[4]),
        pltpu.make_async_copy(slab.at[gx, :, pl.ds(half + 8, 8)], buf_b.at[1, gx], local.at[5]),
    ]
    for copy in copies:
        copy.start()
    mine_all = []
    for p in range(2):
        copies[p].wait()
        three(sa1.at[p], ra1.at[p]).wait_recv()
        for steps in FAR_FIRST:
            second_a(p, steps).start()
        mine = pltpu.make_async_copy(buf_a.at[p, :, gx], plane.at[:, gx, pl.ds(8 * p, 8)], local.at[6 + p])
        mine.start()
        mine_all.append(mine)
        copies[4 + p].wait()
        fifteen(sb1.at[p], rb1.at[p]).wait_recv()
        for i in ORDER:
            second_b(p, i).start()
        mine = pltpu.make_async_copy(buf_b.at[p, :, gy], plane.at[gy, :, pl.ds(half + 8 * p, 8)], local.at[8 + p])
        mine.start()
        mine_all.append(mine)
    for i in ORDER:
        factor_y(i, gy).start()
    loop(1, n_gx // 2, lambda i: factor_x(i, chip).start())
    for p in range(2):
        fifteen(sa2.at[p], ra2.at[p]).wait_recv()
        three(sb2.at[p], rb2.at[p]).wait_recv()
    for mine in mine_all:
        mine.wait()

    for g in range(n_gy):
        p_high[g], p_low[g] = split(plane[g].reshape(512, 128))
    joined = lambda ref: jnp.concatenate([ref[g] for g in range(n_gy)], axis=1)

    def x_rows(q0, q1):
        parts = []
        for q in (q0, q1):
            rows = plane[:, :, pl.ds(pl.multiple_of(q * 8, 8), 8), :].reshape(n_gy, 128, 128)
            parts.append(jnp.concatenate([rows[g] for g in range(n_gy)], axis=1))
        rows = split(jnp.concatenate(parts, axis=0))
        return dot3(rows, (joined(p_high), joined(p_low)), ((1,), (1,)))

    def y_rows(q0, q1):
        rows = [jnp.concatenate([ref[q0], ref[q1]], axis=1) for ref in (p_high, p_low)]
        return dot3(rows, (joined(p_high), joined(p_low)), ((0,), (0,)))

    def x_part(i, slot, h):
        t = step(gy, i)
        return remote(total.at[t, h], got1.at[slot, h], s1.at[i, h], r1.at[slot, h], {"gy": t})

    def y_part(i, slot, h):
        t = step(x, i)
        return remote(total.at[t, h], got1.at[slot, h], s1.at[i, h], r1.at[slot, h], chip_at(t, y, gy))

    def x_half(rows, h):
        columns = rows[:, 256 * h : 256 * h + 256]
        return jnp.concatenate([columns[0:64], columns[64:128]], axis=1)

    def y_half(rows, h):
        return rows.reshape(4, 2, 16, 512)[:, h].reshape(64, 512)

    def swap(q):
        return remote(to_sib.at[q], got0.at[q], s0.at[q], r0.at[q], sibling)

    def grams(theirs, their_q, mine, my_q, part, half_of):
        for pair in ((2, 1), (3, 0)):
            value = theirs(step(their_q, pair[0]), step(their_q, pair[1]))
            for k, i in enumerate(pair):
                q = step(their_q, i)
                to_sib[q] = value[128 * k : 128 * k + 128]
                swap(q).start()
        def own(pair):
            value = mine(step(my_q, pair[0]), step(my_q, pair[1]))
            for k, i in enumerate(pair):
                q = step(my_q, i)
                swap(q).wait_recv()
                rows = value[128 * k : 128 * k + 128] + got0[q]
                for h in range(2):
                    total[q, h] = half_of(rows, h)

        own((2, 1))
        part(2, my_q, 0).start()
        part(1, my_q, 0).start()
        own((3, 0))
        for i, h in ((3, 0), (2, 1), (1, 1), (3, 1)):
            part(i, my_q, h).start()

    @pl.when(core == 0)
    def _():
        grams(y_rows, x, x_rows, gy, x_part, x_half)

    @pl.when(core == 1)
    def _():
        grams(x_rows, gy, y_rows, x, y_part, y_half)

    copies[2].wait()
    copies[3].wait()
    for i in (1, 3, 2):
        factor_y(i, along_y(i)).wait()
    share(fy_all, 0, core).start()
    loop(1, n_gx // 2, lambda i: factor_x(i, lax.rem(chip + i, n_gx // 2)).wait())
    share(fx_all, 1, core).start()
    share(fy_all, 0, 1 - core).wait()
    whole = (joined(p_high), joined(p_low))
    inner = split(dot3(whole, split(fy_all[...].reshape(512, 256)), ((1,), (0,))))
    share(fx_all, 1, 1 - core).wait()
    product = dot3(split(fx_all[...].reshape(512, 256)), inner, ((0,), (0,)))
    product = product.reshape(n_gx, 2, 8, 256)
    upper, lower = product[:, 0].reshape(128, 256), product[:, 1].reshape(128, 256)
    lane = lax.broadcasted_iota(jnp.int32, (128, 128), 1)
    for g in range(n_gy):
        j = g // 2 * 128
        left, right = upper[:, j : j + 128], lower[:, j : j + 128]
        if g % 2 == 0:
            right = pltpu.roll(right, 64, 1)
        else:
            left = pltpu.roll(left, 64, 1)
        tiles[g] = jnp.where(lane < 64, left, right)

    def out1(i, slot):
        t = along_y(i)
        return remote(tiles.at[t], mid.at[slot], sc1.at[i], rc1.at[slot], {"gy": t})

    for i in ORDER:
        out1(i, gy).start()
    mine1 = pltpu.make_async_copy(tiles.at[gy], mid.at[gy], local.at[0])
    mine1.start()

    def x_piece(steps, slot, h):
        to_x, to_y = step(x, steps[0]), step(y, steps[1])
        src = part1.at[h, (lax.rem(to_y, 2) * 4 + to_x) * 2 + to_y // 2]
        return remote(src, got2.at[h, slot], s2.at[h], r2.at[h], chip_at(to_x, to_y, gy))

    def y_piece(steps, slot, h):
        to_z, to_y = step(gy, steps[0]), step(y, steps[1])
        return remote(part1.at[h, to_z * 4 + to_y], got2.at[h, slot], s2.at[h], r2.at[h], chip_at(x, to_y, to_z))

    def pieces(h):
        return bytes_of(got2.at[h, pl.ds(0, 15)], s2.at[h], r2.at[h])

    def to_plane(k, slot):
        to_x, to_y = step(x, FAR_PAIRS[k][0]), step(y, FAR_PAIRS[k][1])
        dst = gram_y_t.at[slot]
        return remote(dst, dst, s4.at[k], r4.at[slot], chip_at(to_x, to_y, gy))

    def sum_parts(part, own, h):
        for i in (1, 3, 2):
            part(i, step(own, i), h).wait()
        return (total[own, h] + got1[step(own, 2), h]) + (got1[step(own, 1), h] + got1[step(own, 3), h])

    @pl.when(core == 0)
    def _():
        for h in range(2):
            rows = sum_parts(x_part, gy, h)
            rows = jnp.concatenate([rows[:, 0:256], rows[:, 256:512]], axis=0).reshape(8, 2, 8, 256)
            even, odd = rows[:, 0].reshape(64, 256), rows[:, 1].reshape(64, 256)
            sub = lax.rem(lax.broadcasted_iota(jnp.int32, (64, 256), 0), 8)
            low = jnp.where(sub < 4, even, pltpu.roll(odd, 4, 0)).reshape(8, 8, 256)
            high = jnp.where(sub < 4, pltpu.roll(even, 60, 0), odd).reshape(8, 8, 256)
            by_tile = part1.reshape(2, 8, 2, 2, 8, 128)
            for t in range(2):
                by_tile[h, :, 0, t] = low[:, :, 128 * t : 128 * t + 128]
                by_tile[h, :, 1, t] = high[:, :, 128 * t : 128 * t + 128]
            me = x * 4 + y
            for steps in FAR_PAIRS:
                x_piece(steps, me, h).start()

    @pl.when(core == 1)
    def _():
        for h in range(2):
            rows = sum_parts(y_part, x, h)
            for z in range(4):
                part1[h, 4 * z : 4 * z + 4] = rows[:, 128 * z : 128 * z + 128].reshape(4, 16, 128)
            me = gy * 4 + y
            for steps in FAR_PAIRS:
                y_piece(steps, me, h).start()

    mine1.wait()
    for i in (1, 3, 2):
        out1(i, along_y(i)).wait()
    mid4 = mid.reshape(n_gy, n_gx, 8, 128)

    def out2(i, owner):
        t = along_x(i)
        return remote(mid4.at[:, t], core_tiles.at[owner], sc2.at[i], rc2.at[owner], {"gx": t})

    loop(1, n_gx, lambda i: out2(i, gx).start())
    mine2 = pltpu.make_async_copy(mid4.at[:, gx], core_tiles.at[gx], local.at[1])
    mine2.start()

    to_sibling = remote(part2, last, s4.at[15], r4.at[16], sibling)
    all_rows = remote(gram_y_t, gram_y_t, s4.at[15], r4.at[17], sibling)

    def hand_over(j):
        return remote(gram_y_t.at[j], gram_y_t.at[j], s4.at[15], r4.at[17], sibling)


    @pl.when(core == 0)
    def _():
        me = x * 4 + y
        for h in range(2):
            pieces(h).wait()
            got2[h, me] = part1[h, (y_lo * 4 + x) * 2 + sa]
            part2[16 * h : 16 * h + 16] = jnp.sum(got2[h], axis=0) * scale
        to_sibling.start()
        for t in range(4):
            gram_x[:, 128 * t : 128 * t + 128] = part2[8 * t : 8 * t + 4]
        to_sibling.wait_send()
        all_rows.wait_recv()

    @pl.when(core == 1)
    def _():
        me = gy * 4 + y
        here = x * 4 + y
        for h in range(2):
            pieces(h).wait()
            got2[h, me] = part1[h, me]
            gram_y_t[here, 16 * h : 16 * h + 16] = jnp.sum(got2[h], axis=0) * scale
        for k in range(15):
            to_plane(k, here).start()
        to_sibling.wait_recv()
        for t in range(4):
            gram_x[:, 128 * t : 128 * t + 128] = last[8 * t + 4 : 8 * t + 8]
        hand_over(here).start()
        for k in range(14, -1, -1):
            j = step(x, FAR_PAIRS[k][0]) * 4 + step(y, FAR_PAIRS[k][1])
            to_plane(k, j).wait_recv()
            hand_over(j).start()
        for k in range(15):
            to_plane(k, here).wait_send()
        all_rows.wait_send()

    mine2.wait()
    loop(1, n_gx, lambda i: out2(i, along_x(i)).wait())
    loop(0, 4, lambda q: swap(q).wait_send())
    for p in range(2):
        three(sa1.at[p], ra1.at[p]).wait_send()
        fifteen(sb1.at[p], rb1.at[p]).wait_send()
        fifteen(sa2.at[p], ra2.at[p]).wait_send()
        three(sb2.at[p], rb2.at[p]).wait_send()


def finish_kernel(gx_in, gy_in, core_in, gx_out, gy_out, core_out):
    gx_out[...] = gx_in[...]
    gy_out[...] = gy_in[...].reshape(512, 128).T
    tile = core_in[...].reshape(64, 8, 128)
    core_out[:, 0:8, :] = tile[:, :, 0:64]
    core_out[:, 8:16, :] = tile[:, :, 64:128]


def shards(slab, factor_x, factor_y):
    z_cells, s_local, x_local, y_local = slab.shape
    n_gx, n_gy, n_sa = lax.axis_size("gx"), lax.axis_size("gy"), lax.axis_size("sa")
    scale = 1.0 / (y_local * n_gy * z_cells * s_local * n_sa)
    rank = factor_x.shape[1]
    vmem = pltpu.VMEM
    results = pl.pallas_call(
        functools.partial(tucker_kernel, scale),
        out_shape=(
            jax.ShapeDtypeStruct((4, 512), F32),
            jax.ShapeDtypeStruct((16, 32, 128), F32),
            jax.ShapeDtypeStruct((n_gx, n_gy, 8, 128), F32),
        ),
        in_specs=[HBM] * 3,
        out_specs=(VMEM,) * 3,
        scratch_shapes=[
            vmem((2, 4, 16, 8, 128), F32), vmem((2, 16, 4, 8, 128), F32), vmem((4, 16, 32, 128), F32),
            vmem((8, 2, 32, 256), F32), vmem((4, 2, 64, 256), F32),
            vmem((4, 512, 128), BF16), vmem((4, 512, 128), BF16),
            vmem((4, 128, 512), F32), vmem((4, 128, 512), F32), vmem((4, 2, 64, 512), F32), vmem((4, 2, 64, 512), F32),
            vmem((2, 16, 16, 128), F32), vmem((2, 16, 16, 128), F32), vmem((32, 128), F32), vmem((32, 128), F32),
            vmem((4, 128, 128), F32), vmem((4, 128, 128), F32),
            DMA((2,)), DMA((2,)), DMA((2,)), DMA((2,)), DMA((2,)), DMA((2,)), DMA((2,)), DMA((2,)),
            DMA((8,)), DMA((8,)), DMA((4,)), DMA((4,)), DMA((2,)), DMA((2,)),
            DMA((4,)), DMA((4,)), DMA((4, 2)), DMA((4, 2)), DMA((2,)), DMA((2,)), DMA((16,)), DMA((18,)),
            DMA((4,)), DMA((4,)), DMA((16,)), DMA((16,)), DMA((10,)),
        ],
        compiler_params=pltpu.CompilerParams(collective_id=0, has_side_effects=True, vmem_limit_bytes=40 << 20),
        name="tucker",
    )(
        *(pltpu.with_memory_space_constraint(v, pltpu.HBM) for v in (
            slab.reshape(n_gx, n_gy, x_local, y_local), factor_x, factor_y.reshape(2, y_local // 2, rank)))
    )
    gram_x, gram_y, core = pl.pallas_call(
        finish_kernel,
        out_shape=(
            jax.ShapeDtypeStruct((4, 512), F32),
            jax.ShapeDtypeStruct((128, 512), F32),
            jax.ShapeDtypeStruct((64, 16, 64), F32),
        ),
        in_specs=[VMEM] * 3,
        out_specs=(VMEM,) * 3,
        compiler_params=pltpu.CompilerParams(vmem_limit_bytes=40 << 20),
        name="finish",
    )(*results)
    return gram_x, gram_y, core.reshape(z_cells, s_local, rank // n_gx, rank // n_gy)


def solution(mesh):
    in_specs = (P(None, "sa", "gx", "gy"), P("gx", None), P("gy", None))
    out_specs = (P(("gx", "gy", "sa"), None), P("gy", None), P(None, "sa", "gx", "gy"))
    return jax.shard_map(shards, mesh=mesh, in_specs=in_specs, out_specs=out_specs, check_vma=False)
```

```python
import functools

import jax
import jax.numpy as jnp
from jax import lax
from jax.experimental import pallas as pl
from jax.experimental.pallas import tpu as pltpu
from jax.sharding import PartitionSpec as P

MESH = pl.DeviceIdType.MESH
DMA = pltpu.SemaphoreType.DMA
F32 = jnp.float32
BF16 = jnp.bfloat16
VMEM = pl.BlockSpec(memory_space=pltpu.VMEM)
HBM = pl.BlockSpec(memory_space=pltpu.HBM)
ORDER = (2, 1, 3)
FAR_PAIRS = (
    (2, 2), (2, 1), (1, 2), (2, 3), (3, 2), (1, 1), (3, 3), (1, 3), (3, 1), (2, 0), (0, 2), (1, 0), (0, 1), (3, 0), (0, 3),
)
FAR_FIRST = (
    (2, 1, 0), (2, 1, 1), (1, 1, 0), (3, 1, 1), (2, 0, 0), (0, 1, 0), (1, 1, 1), (3, 1, 0),
    (2, 0, 1), (0, 1, 1), (1, 0, 0), (3, 0, 0), (1, 0, 1), (3, 0, 1), (0, 0, 1),
)


def loop(start, stop, body):
    def step(i, carry):
        body(i)
        return carry

    lax.fori_loop(start, stop, step, 0)


def remote(src, dst, send, recv, device):
    return pltpu.make_async_remote_copy(
        src_ref=src, dst_ref=dst, send_sem=send, recv_sem=recv, device_id=device, device_id_type=MESH
    )


def greet(devices_of, count):
    barrier = pltpu.get_barrier_semaphore()
    loop(1, count, lambda i: pl.semaphore_signal(barrier, 1, device_id=devices_of(i), device_id_type=MESH))


def split(value):
    high = value.astype(BF16)
    return high, (value - high.astype(F32)).astype(BF16)


def dot3(a, b, dims):
    (a_high, a_low), (b_high, b_low) = a, b
    dot = lambda p, q: lax.dot_general(p, q, (dims, ((), ())), preferred_element_type=F32)
    return dot(a_high, b_low) + dot(a_low, b_high) + dot(a_high, b_high)


def tucker_kernel(
    scale, slab, fx, fy, gram_x, gram_y_t, core_tiles,
    buf_a, buf_b, plane, fx_all, fy_all, p_high, p_low, to_sib, got0, total, got1, part1, got2, part2, last, tiles, mid,
    sa1, ra1, sa2, ra2, sb1, rb1, sb2, rb2, sfx, rfx, sfy, rfy, ss, rs,
    s0, r0, s1, r1, s2, r2, s4, r4, sc1, rc1, sc2, rc2, local,
):
    gx, gy, sa = lax.axis_index("gx"), lax.axis_index("gy"), lax.axis_index("sa")
    n_gx, n_gy = 16, 4
    chip, core = gx // 2, lax.rem(gx, 2)
    x, y_lo = lax.rem(chip, 4), chip // 4
    y = sa * 2 + y_lo
    half = 16
    step = lambda v, i: lax.rem(v + i, 4)
    along_x = lambda i: lax.rem(gx + i, n_gx)
    along_y = lambda i: lax.rem(gy + i, n_gy)
    sibling = {"gx": gx + 1 - 2 * core}

    def chip_at(to_x, to_y, to_z):
        return {"gx": lax.rem(to_y, 2) * 8 + to_x * 2 + core, "gy": to_z, "sa": to_y // 2}

    barrier = pltpu.get_barrier_semaphore()
    greet(lambda i: {"gx": along_x(i)}, n_gx)
    greet(lambda i: {"gy": along_y(i)}, n_gy)
    loop(0, 8, lambda i: pl.semaphore_signal(
        barrier, 1, device_id={"gx": i * 2 + core, "sa": 1 - sa}, device_id_type=MESH))

    @pl.when(core == 1)
    def _():
        for i in (1, 2, 3):
            for j in (1, 2, 3):
                pl.semaphore_signal(barrier, 1, device_id=chip_at(x, step(y, i), step(gy, j)), device_id_type=MESH)

    pl.semaphore_wait(barrier, n_gx + n_gy - 2 + 8 + 9 * core)

    def near(steps):
        dx, dy, dc = steps
        return lax.rem(y_lo + dy, 2) * 8 + step(x, dx) * 2 + lax.rem(core + dc, 2)

    def first_a(p, i):
        t = along_y(i)
        return remote(slab.at[:, t, pl.ds(8 * p, 8)], buf_a.at[p, gy], sa1.at[p], ra1.at[p], {"gy": t})

    def first_b(p, steps):
        t = near(steps)
        return remote(slab.at[t, :, pl.ds(half + 8 * p, 8)], buf_b.at[p, gx], sb1.at[p], rb1.at[p], {"gx": t})

    def second_a(p, steps):
        t = near(steps)
        dst = plane.at[:, gx, pl.ds(8 * p, 8)]
        return remote(buf_a.at[p, :, t], dst, sa2.at[p], ra2.at[p], {"gx": t})

    def second_b(p, i):
        t = along_y(i)
        dst = plane.at[gy, :, pl.ds(half + 8 * p, 8)]
        return remote(buf_b.at[p, :, t], dst, sb2.at[p], rb2.at[p], {"gy": t})

    def bytes_of(ref, send, recv):
        return remote(ref, ref, send, recv, sibling)

    three = lambda send, recv: bytes_of(buf_a.at[0, pl.ds(0, 3)], send, recv)
    fifteen = lambda send, recv: bytes_of(buf_b.at[0, pl.ds(0, 15)], send, recv)

    def factor_x(i, owner):
        t = lax.rem(chip + i, n_gx // 2)
        return remote(fx, fx_all.at[owner, core], sfx.at[i], rfx.at[owner], {"gx": t * 2 + core})

    def factor_y(i, owner):
        return remote(fy.at[core], fy_all.at[owner, core], sfy.at[i], rfy.at[owner], {"gy": along_y(i)})

    def share(all_ref, k, side):
        return remote(all_ref.at[:, core], all_ref.at[:, side], ss.at[k], rs.at[k], sibling)

    for p in range(2):
        for i in ORDER:
            first_a(p, i).start()
        for steps in FAR_FIRST:
            first_b(p, steps).start()
    copies = [
        pltpu.make_async_copy(slab.at[:, gy, pl.ds(0, 8)], buf_a.at[0, gy], local.at[0]),
        pltpu.make_async_copy(slab.at[:, gy, pl.ds(8, 8)], buf_a.at[1, gy], local.at[1]),
        pltpu.make_async_copy(fx, fx_all.at[chip, core], local.at[2]),
        pltpu.make_async_copy(fy.at[core], fy_all.at[gy, core], local.at[3]),
        pltpu.make_async_copy(slab.at[gx, :, pl.ds(half, 8)], buf_b.at[0, gx], local.at[4]),
        pltpu.make_async_copy(slab.at[gx, :, pl.ds(half + 8, 8)], buf_b.at[1, gx], local.at[5]),
    ]
    for copy in copies:
        copy.start()
    mine_all = []
    for p in range(2):
        copies[p].wait()
        three(sa1.at[p], ra1.at[p]).wait_recv()
        for steps in FAR_FIRST:
            second_a(p, steps).start()
        mine = pltpu.make_async_copy(buf_a.at[p, :, gx], plane.at[:, gx, pl.ds(8 * p, 8)], local.at[6 + p])
        mine.start()
        mine_all.append(mine)
        copies[4 + p].wait()
        fifteen(sb1.at[p], rb1.at[p]).wait_recv()
        for i in ORDER:
            second_b(p, i).start()
        mine = pltpu.make_async_copy(buf_b.at[p, :, gy], plane.at[gy, :, pl.ds(half + 8 * p, 8)], local.at[8 + p])
        mine.start()
        mine_all.append(mine)
    for i in ORDER:
        factor_y(i, gy).start()
    for i in (6, 2, 5, 7, 3, 1, 4):
        factor_x(i, chip).start()
    for p in range(2):
        fifteen(sa2.at[p], ra2.at[p]).wait_recv()
        three(sb2.at[p], rb2.at[p]).wait_recv()
    for mine in mine_all:
        mine.wait()

    for g in range(n_gy):
        p_high[g], p_low[g] = split(plane[g].reshape(512, 128))
    joined = lambda ref: jnp.concatenate([ref[g] for g in range(n_gy)], axis=1)

    def x_rows(q0, q1):
        parts = []
        for q in (q0, q1):
            rows = plane[:, :, pl.ds(pl.multiple_of(q * 8, 8), 8), :].reshape(n_gy, 128, 128)
            parts.append(jnp.concatenate([rows[g] for g in range(n_gy)], axis=1))
        rows = split(jnp.concatenate(parts, axis=0))
        return dot3(rows, (joined(p_high), joined(p_low)), ((1,), (1,)))

    def y_rows(q0, q1):
        rows = [jnp.concatenate([ref[q0], ref[q1]], axis=1) for ref in (p_high, p_low)]
        return dot3(rows, (joined(p_high), joined(p_low)), ((0,), (0,)))

    def x_part(i, slot, h):
        t = step(gy, i)
        return remote(total.at[t, h], got1.at[slot, h], s1.at[i, h], r1.at[slot, h], {"gy": t})

    def y_part(i, slot, h):
        t = step(x, i)
        return remote(total.at[t, h], got1.at[slot, h], s1.at[i, h], r1.at[slot, h], chip_at(t, y, gy))

    def x_half(rows, h):
        columns = rows[:, 256 * h : 256 * h + 256]
        return jnp.concatenate([columns[0:64], columns[64:128]], axis=1)

    def y_half(rows, h):
        return rows.reshape(4, 2, 16, 512)[:, h].reshape(64, 512)

    def swap(q):
        return remote(to_sib.at[q], got0.at[q], s0.at[q], r0.at[q], sibling)

    def grams(theirs, their_q, mine, my_q, part, half_of):
        for pair in ((2, 1), (3, 0)):
            value = theirs(step(their_q, pair[0]), step(their_q, pair[1]))
            for k, i in enumerate(pair):
                q = step(their_q, i)
                to_sib[q] = value[128 * k : 128 * k + 128]
                swap(q).start()
        def own(pair):
            value = mine(step(my_q, pair[0]), step(my_q, pair[1]))
            for k, i in enumerate(pair):
                q = step(my_q, i)
                swap(q).wait_recv()
                rows = value[128 * k : 128 * k + 128] + got0[q]
                for h in range(2):
                    total[q, h] = half_of(rows, h)

        own((2, 1))
        part(2, my_q, 0).start()
        part(1, my_q, 0).start()
        own((3, 0))
        for i, h in ((3, 0), (2, 1), (1, 1), (3, 1)):
            part(i, my_q, h).start()

    @pl.when(core == 0)
    def _():
        grams(y_rows, x, x_rows, gy, x_part, x_half)

    @pl.when(core == 1)
    def _():
        grams(x_rows, gy, y_rows, x, y_part, y_half)

    copies[2].wait()
    copies[3].wait()
    for i in (1, 3, 2):
        factor_y(i, along_y(i)).wait()
    share(fy_all, 0, core).start()
    loop(1, n_gx // 2, lambda i: factor_x(i, lax.rem(chip + i, n_gx // 2)).wait())
    share(fx_all, 1, core).start()
    share(fy_all, 0, 1 - core).wait()
    whole = (joined(p_high), joined(p_low))
    inner = split(dot3(whole, split(fy_all[...].reshape(512, 256)), ((1,), (0,))))
    share(fx_all, 1, 1 - core).wait()
    product = dot3(split(fx_all[...].reshape(512, 256)), inner, ((0,), (0,)))
    product = product.reshape(n_gx, 2, 8, 256)
    upper, lower = product[:, 0].reshape(128, 256), product[:, 1].reshape(128, 256)
    lane = lax.broadcasted_iota(jnp.int32, (128, 128), 1)
    for g in range(n_gy):
        j = g // 2 * 128
        left, right = upper[:, j : j + 128], lower[:, j : j + 128]
        if g % 2 == 0:
            right = pltpu.roll(right, 64, 1)
        else:
            left = pltpu.roll(left, 64, 1)
        tiles[g] = jnp.where(lane < 64, left, right)

    def out1(i, slot):
        t = along_y(i)
        return remote(tiles.at[t], mid.at[slot], sc1.at[i], rc1.at[slot], {"gy": t})

    for i in ORDER:
        out1(i, gy).start()
    mine1 = pltpu.make_async_copy(tiles.at[gy], mid.at[gy], local.at[0])
    mine1.start()

    def x_piece(steps, slot, h):
        to_x, to_y = step(x, steps[0]), step(y, steps[1])
        src = part1.at[h, (lax.rem(to_y, 2) * 4 + to_x) * 2 + to_y // 2]
        return remote(src, got2.at[h, slot], s2.at[h], r2.at[h], chip_at(to_x, to_y, gy))

    def y_piece(steps, slot, h):
        to_z, to_y = step(gy, steps[0]), step(y, steps[1])
        return remote(part1.at[h, to_z * 4 + to_y], got2.at[h, slot], s2.at[h], r2.at[h], chip_at(x, to_y, to_z))

    def pieces(h):
        return bytes_of(got2.at[h, pl.ds(0, 15)], s2.at[h], r2.at[h])

    def to_plane(k, slot, h):
        to_x, to_y = step(x, FAR_PAIRS[k][0]), step(y, FAR_PAIRS[k][1])
        dst = gram_y_t.at[slot, pl.ds(16 * h, 16)]
        return remote(dst, dst, s4.at[h, k], r4.at[h, slot], chip_at(to_x, to_y, gy))

    def sum_parts(part, own, h):
        for i in (1, 3, 2):
            part(i, step(own, i), h).wait()
        return (total[own, h] + got1[step(own, 2), h]) + (got1[step(own, 1), h] + got1[step(own, 3), h])

    @pl.when(core == 0)
    def _():
        for h in range(2):
            rows = sum_parts(x_part, gy, h)
            rows = jnp.concatenate([rows[:, 0:256], rows[:, 256:512]], axis=0).reshape(8, 2, 8, 256)
            even, odd = rows[:, 0].reshape(64, 256), rows[:, 1].reshape(64, 256)
            sub = lax.rem(lax.broadcasted_iota(jnp.int32, (64, 256), 0), 8)
            low = jnp.where(sub < 4, even, pltpu.roll(odd, 4, 0)).reshape(8, 8, 256)
            high = jnp.where(sub < 4, pltpu.roll(even, 60, 0), odd).reshape(8, 8, 256)
            by_tile = part1.reshape(2, 8, 2, 2, 8, 128)
            for t in range(2):
                by_tile[h, :, 0, t] = low[:, :, 128 * t : 128 * t + 128]
                by_tile[h, :, 1, t] = high[:, :, 128 * t : 128 * t + 128]
            me = x * 4 + y
            for steps in FAR_PAIRS:
                x_piece(steps, me, h).start()

    @pl.when(core == 1)
    def _():
        for h in range(2):
            rows = sum_parts(y_part, x, h)
            for z in range(4):
                part1[h, 4 * z : 4 * z + 4] = rows[:, 128 * z : 128 * z + 128].reshape(4, 16, 128)
            me = gy * 4 + y
            for steps in FAR_PAIRS:
                y_piece(steps, me, h).start()

    mine1.wait()
    for i in (1, 3, 2):
        out1(i, along_y(i)).wait()
    mid4 = mid.reshape(n_gy, n_gx, 8, 128)

    for steps in FAR_FIRST:
        t = near(steps)
        remote(mid4.at[:, t], core_tiles.at[gx], sc2.at[0], rc2.at[0], {"gx": t}).start()
    mine2 = pltpu.make_async_copy(mid4.at[:, gx], core_tiles.at[gx], local.at[1])
    mine2.start()

    to_sibling = remote(part2, last, s4.at[0, 15], r4.at[0, 16], sibling)
    all_rows = remote(gram_y_t, gram_y_t, s4.at[0, 15], r4.at[0, 17], sibling)

    def hand_over(j, h):
        rows = gram_y_t.at[j, pl.ds(16 * h, 16)]
        return remote(rows, rows, s4.at[0, 15], r4.at[0, 17], sibling)


    @pl.when(core == 0)
    def _():
        me = x * 4 + y
        for h in range(2):
            pieces(h).wait()
            got2[h, me] = part1[h, (y_lo * 4 + x) * 2 + sa]
            part2[16 * h : 16 * h + 16] = jnp.sum(got2[h], axis=0) * scale
        to_sibling.start()
        for t in range(4):
            gram_x[:, 128 * t : 128 * t + 128] = part2[8 * t : 8 * t + 4]
        to_sibling.wait_send()
        all_rows.wait_recv()

    @pl.when(core == 1)
    def _():
        me = gy * 4 + y
        here = x * 4 + y
        for h in range(2):
            pieces(h).wait()
            got2[h, me] = part1[h, me]
            gram_y_t[here, 16 * h : 16 * h + 16] = jnp.sum(got2[h], axis=0) * scale
            for k in range(15):
                to_plane(k, here, h).start()
            hand_over(here, h).start()
        to_sibling.wait_recv()
        for t in range(4):
            gram_x[:, 128 * t : 128 * t + 128] = last[8 * t + 4 : 8 * t + 8]
        for h in range(2):
            for k in range(14, -1, -1):
                j = step(x, FAR_PAIRS[k][0]) * 4 + step(y, FAR_PAIRS[k][1])
                to_plane(k, j, h).wait_recv()
                hand_over(j, h).start()
        for h in range(2):
            for k in range(15):
                to_plane(k, here, h).wait_send()
        all_rows.wait_send()

    mine2.wait()
    bytes_of(core_tiles.at[pl.ds(0, 15)], sc2.at[0], rc2.at[0]).wait()
    loop(0, 4, lambda q: swap(q).wait_send())
    for p in range(2):
        three(sa1.at[p], ra1.at[p]).wait_send()
        fifteen(sb1.at[p], rb1.at[p]).wait_send()
        fifteen(sa2.at[p], ra2.at[p]).wait_send()
        three(sb2.at[p], rb2.at[p]).wait_send()


def finish_kernel(gx_in, gy_in, core_in, gx_out, gy_out, core_out):
    gx_out[...] = gx_in[...]
    gy_out[...] = gy_in[...].reshape(512, 128).T
    tile = core_in[...].reshape(64, 8, 128)
    core_out[:, 0:8, :] = tile[:, :, 0:64]
    core_out[:, 8:16, :] = tile[:, :, 64:128]


def shards(slab, factor_x, factor_y):
    z_cells, s_local, x_local, y_local = slab.shape
    n_gx, n_gy, n_sa = lax.axis_size("gx"), lax.axis_size("gy"), lax.axis_size("sa")
    scale = 1.0 / (y_local * n_gy * z_cells * s_local * n_sa)
    rank = factor_x.shape[1]
    vmem = pltpu.VMEM
    results = pl.pallas_call(
        functools.partial(tucker_kernel, scale),
        out_shape=(
            jax.ShapeDtypeStruct((4, 512), F32),
            jax.ShapeDtypeStruct((16, 32, 128), F32),
            jax.ShapeDtypeStruct((n_gx, n_gy, 8, 128), F32),
        ),
        in_specs=[HBM] * 3,
        out_specs=(VMEM,) * 3,
        scratch_shapes=[
            vmem((2, 4, 16, 8, 128), F32), vmem((2, 16, 4, 8, 128), F32), vmem((4, 16, 32, 128), F32),
            vmem((8, 2, 32, 256), F32), vmem((4, 2, 64, 256), F32),
            vmem((4, 512, 128), BF16), vmem((4, 512, 128), BF16),
            vmem((4, 128, 512), F32), vmem((4, 128, 512), F32), vmem((4, 2, 64, 512), F32), vmem((4, 2, 64, 512), F32),
            vmem((2, 16, 16, 128), F32), vmem((2, 16, 16, 128), F32), vmem((32, 128), F32), vmem((32, 128), F32),
            vmem((4, 128, 128), F32), vmem((4, 128, 128), F32),
            DMA((2,)), DMA((2,)), DMA((2,)), DMA((2,)), DMA((2,)), DMA((2,)), DMA((2,)), DMA((2,)),
            DMA((8,)), DMA((8,)), DMA((4,)), DMA((4,)), DMA((2,)), DMA((2,)),
            DMA((4,)), DMA((4,)), DMA((4, 2)), DMA((4, 2)), DMA((2,)), DMA((2,)), DMA((2, 16)), DMA((2, 18)),
            DMA((4,)), DMA((4,)), DMA((16,)), DMA((16,)), DMA((10,)),
        ],
        compiler_params=pltpu.CompilerParams(collective_id=0, has_side_effects=True, vmem_limit_bytes=40 << 20),
        name="tucker",
    )(
        *(pltpu.with_memory_space_constraint(v, pltpu.HBM) for v in (
            slab.reshape(n_gx, n_gy, x_local, y_local), factor_x, factor_y.reshape(2, y_local // 2, rank)))
    )
    gram_x, gram_y, core = pl.pallas_call(
        finish_kernel,
        out_shape=(
            jax.ShapeDtypeStruct((4, 512), F32),
            jax.ShapeDtypeStruct((128, 512), F32),
            jax.ShapeDtypeStruct((64, 16, 64), F32),
        ),
        in_specs=[VMEM] * 3,
        out_specs=(VMEM,) * 3,
        compiler_params=pltpu.CompilerParams(vmem_limit_bytes=40 << 20),
        name="finish",
    )(*results)
    return gram_x, gram_y, core.reshape(z_cells, s_local, rank // n_gx, rank // n_gy)


def solution(mesh):
    in_specs = (P(None, "sa", "gx", "gy"), P("gx", None), P("gy", None))
    out_specs = (P(("gx", "gy", "sa"), None), P("gy", None), P(None, "sa", "gx", "gy"))
    return jax.shard_map(shards, mesh=mesh, in_specs=in_specs, out_specs=out_specs, check_vma=False)
```

```python
import functools

import jax
import jax.numpy as jnp
from jax import lax
from jax.experimental import pallas as pl
from jax.experimental.pallas import tpu as pltpu
from jax.sharding import PartitionSpec as P

MESH = pl.DeviceIdType.MESH
DMA = pltpu.SemaphoreType.DMA
F32 = jnp.float32
BF16 = jnp.bfloat16
VMEM = pl.BlockSpec(memory_space=pltpu.VMEM)
HBM = pl.BlockSpec(memory_space=pltpu.HBM)
ORDER = (2, 1, 3)
FAR_PAIRS = (
    (2, 2), (2, 1), (1, 2), (2, 3), (3, 2), (1, 1), (3, 3), (1, 3), (3, 1), (2, 0), (0, 2), (1, 0), (0, 1), (3, 0), (0, 3),
)
FAR_FIRST = (
    (2, 1, 0), (2, 1, 1), (1, 1, 0), (3, 1, 1), (2, 0, 0), (0, 1, 0), (1, 1, 1), (3, 1, 0),
    (2, 0, 1), (0, 1, 1), (1, 0, 0), (3, 0, 0), (1, 0, 1), (3, 0, 1), (0, 0, 1),
)


def loop(start, stop, body):
    def step(i, carry):
        body(i)
        return carry

    lax.fori_loop(start, stop, step, 0)


def remote(src, dst, send, recv, device):
    return pltpu.make_async_remote_copy(
        src_ref=src, dst_ref=dst, send_sem=send, recv_sem=recv, device_id=device, device_id_type=MESH
    )


def greet(devices_of, count):
    barrier = pltpu.get_barrier_semaphore()
    loop(1, count, lambda i: pl.semaphore_signal(barrier, 1, device_id=devices_of(i), device_id_type=MESH))


def split(value):
    high = value.astype(BF16)
    return high, (value - high.astype(F32)).astype(BF16)


def dot3(a, b, dims):
    (a_high, a_low), (b_high, b_low) = a, b
    dot = lambda p, q: lax.dot_general(p, q, (dims, ((), ())), preferred_element_type=F32)
    return dot(a_high, b_low) + dot(a_low, b_high) + dot(a_high, b_high)


def tucker_kernel(
    scale, slab, fx, fy, gram_x, gram_y_t, core_tiles,
    buf_a, buf_b, plane, fx_all, fy_all, p_high, p_low, to_sib, got0, total, got1, part1, got2, part2, last, tiles, mid,
    sa1, ra1, sa2, ra2, sb1, rb1, sb2, rb2, sfx, rfx, sfy, rfy, ss, rs,
    s0, r0, s1, r1, s2, r2, s4, r4, sc1, rc1, sc2, rc2, local,
):
    gx, gy, sa = lax.axis_index("gx"), lax.axis_index("gy"), lax.axis_index("sa")
    n_gx, n_gy = 16, 4
    chip, core = gx // 2, lax.rem(gx, 2)
    x, y_lo = lax.rem(chip, 4), chip // 4
    y = sa * 2 + y_lo
    half = 16
    step = lambda v, i: lax.rem(v + i, 4)
    along_x = lambda i: lax.rem(gx + i, n_gx)
    along_y = lambda i: lax.rem(gy + i, n_gy)
    sibling = {"gx": gx + 1 - 2 * core}

    def chip_at(to_x, to_y, to_z):
        return {"gx": lax.rem(to_y, 2) * 8 + to_x * 2 + core, "gy": to_z, "sa": to_y // 2}

    barrier = pltpu.get_barrier_semaphore()
    greet(lambda i: {"gx": along_x(i)}, n_gx)
    greet(lambda i: {"gy": along_y(i)}, n_gy)
    loop(0, 8, lambda i: pl.semaphore_signal(
        barrier, 1, device_id={"gx": i * 2 + core, "sa": 1 - sa}, device_id_type=MESH))

    @pl.when(core == 1)
    def _():
        for i in (1, 2, 3):
            for j in (1, 2, 3):
                pl.semaphore_signal(barrier, 1, device_id=chip_at(x, step(y, i), step(gy, j)), device_id_type=MESH)

    pl.semaphore_wait(barrier, n_gx + n_gy - 2 + 8 + 9 * core)

    def near(steps):
        dx, dy, dc = steps
        return lax.rem(y_lo + dy, 2) * 8 + step(x, dx) * 2 + lax.rem(core + dc, 2)

    def first_a(p, i):
        t = along_y(i)
        return remote(slab.at[:, t, pl.ds(8 * p, 8)], buf_a.at[p, gy], sa1.at[p], ra1.at[p], {"gy": t})

    def first_b(p, steps):
        t = near(steps)
        return remote(slab.at[t, :, pl.ds(half + 8 * p, 8)], buf_b.at[p, gx], sb1.at[p], rb1.at[p], {"gx": t})

    def second_a(p, steps):
        t = near(steps)
        dst = plane.at[:, gx, pl.ds(8 * p, 8)]
        return remote(buf_a.at[p, :, t], dst, sa2.at[p], ra2.at[p], {"gx": t})

    def second_b(p, i):
        t = along_y(i)
        dst = plane.at[gy, :, pl.ds(half + 8 * p, 8)]
        return remote(buf_b.at[p, :, t], dst, sb2.at[p], rb2.at[p], {"gy": t})

    def bytes_of(ref, send, recv):
        return remote(ref, ref, send, recv, sibling)

    three = lambda send, recv: bytes_of(buf_a.at[0, pl.ds(0, 3)], send, recv)
    fifteen = lambda send, recv: bytes_of(buf_b.at[0, pl.ds(0, 15)], send, recv)

    def factor_x(i, owner):
        t = lax.rem(chip + i, n_gx // 2)
        return remote(fx, fx_all.at[owner, core], sfx.at[i], rfx.at[owner], {"gx": t * 2 + core})

    def factor_y(i, owner):
        return remote(fy.at[core], fy_all.at[owner, core], sfy.at[i], rfy.at[owner], {"gy": along_y(i)})

    def share(all_ref, k, side):
        return remote(all_ref.at[:, core], all_ref.at[:, side], ss.at[k], rs.at[k], sibling)

    for p in range(2):
        for i in ORDER:
            first_a(p, i).start()
        for steps in FAR_FIRST:
            first_b(p, steps).start()
    copies = [
        pltpu.make_async_copy(slab.at[:, gy, pl.ds(0, 8)], buf_a.at[0, gy], local.at[0]),
        pltpu.make_async_copy(slab.at[:, gy, pl.ds(8, 8)], buf_a.at[1, gy], local.at[1]),
        pltpu.make_async_copy(fx, fx_all.at[chip, core], local.at[2]),
        pltpu.make_async_copy(fy.at[core], fy_all.at[gy, core], local.at[3]),
        pltpu.make_async_copy(slab.at[gx, :, pl.ds(half, 8)], buf_b.at[0, gx], local.at[4]),
        pltpu.make_async_copy(slab.at[gx, :, pl.ds(half + 8, 8)], buf_b.at[1, gx], local.at[5]),
    ]
    for copy in copies:
        copy.start()
    mine_all = []
    for p in range(2):
        copies[p].wait()
        three(sa1.at[p], ra1.at[p]).wait_recv()
        for steps in FAR_FIRST:
            second_a(p, steps).start()
        mine = pltpu.make_async_copy(buf_a.at[p, :, gx], plane.at[:, gx, pl.ds(8 * p, 8)], local.at[6 + p])
        mine.start()
        mine_all.append(mine)
        copies[4 + p].wait()
        fifteen(sb1.at[p], rb1.at[p]).wait_recv()
        for i in ORDER:
            second_b(p, i).start()
        mine = pltpu.make_async_copy(buf_b.at[p, :, gy], plane.at[gy, :, pl.ds(half + 8 * p, 8)], local.at[8 + p])
        mine.start()
        mine_all.append(mine)
    for i in ORDER:
        factor_y(i, gy).start()
    for i in (6, 2, 5, 7, 3, 1, 4):
        factor_x(i, chip).start()
    for p in range(2):
        fifteen(sa2.at[p], ra2.at[p]).wait_recv()
        three(sb2.at[p], rb2.at[p]).wait_recv()
    for mine in mine_all:
        mine.wait()

    for g in range(n_gy):
        p_high[g], p_low[g] = split(plane[g].reshape(512, 128))
    joined = lambda ref: jnp.concatenate([ref[g] for g in range(n_gy)], axis=1)

    def x_rows(q0, q1):
        parts = []
        for q in (q0, q1):
            rows = plane[:, :, pl.ds(pl.multiple_of(q * 8, 8), 8), :].reshape(n_gy, 128, 128)
            parts.append(jnp.concatenate([rows[g] for g in range(n_gy)], axis=1))
        rows = split(jnp.concatenate(parts, axis=0))
        return dot3(rows, (joined(p_high), joined(p_low)), ((1,), (1,)))

    def y_rows(q0, q1):
        rows = [jnp.concatenate([ref[q0], ref[q1]], axis=1) for ref in (p_high, p_low)]
        return dot3(rows, (joined(p_high), joined(p_low)), ((0,), (0,)))

    def x_part(i, slot, h):
        t = step(gy, i)
        return remote(total.at[t, h], got1.at[slot, h], s1.at[i, h], r1.at[slot, h], {"gy": t})

    def y_part(i, slot, h):
        t = step(x, i)
        return remote(total.at[t, h], got1.at[slot, h], s1.at[i, h], r1.at[slot, h], chip_at(t, y, gy))

    def x_half(rows, h):
        columns = rows[:, 256 * h : 256 * h + 256]
        return jnp.concatenate([columns[0:64], columns[64:128]], axis=1)

    def y_half(rows, h):
        return rows.reshape(4, 2, 16, 512)[:, h].reshape(64, 512)

    def swap(q):
        return remote(to_sib.at[q], got0.at[q], s0.at[q], r0.at[q], sibling)

    def grams(theirs, their_q, mine, my_q, part, half_of):
        for pair in ((2, 1), (3, 0)):
            value = theirs(step(their_q, pair[0]), step(their_q, pair[1]))
            for k, i in enumerate(pair):
                q = step(their_q, i)
                to_sib[q] = value[128 * k : 128 * k + 128]
                swap(q).start()
        def own(pair):
            value = mine(step(my_q, pair[0]), step(my_q, pair[1]))
            for k, i in enumerate(pair):
                q = step(my_q, i)
                swap(q).wait_recv()
                rows = value[128 * k : 128 * k + 128] + got0[q]
                for h in range(2):
                    total[q, h] = half_of(rows, h)

        own((2, 1))
        part(2, my_q, 0).start()
        part(1, my_q, 0).start()
        own((3, 0))
        for i, h in ((3, 0), (2, 1), (1, 1), (3, 1)):
            part(i, my_q, h).start()

    @pl.when(core == 0)
    def _():
        grams(y_rows, x, x_rows, gy, x_part, x_half)

    @pl.when(core == 1)
    def _():
        grams(x_rows, gy, y_rows, x, y_part, y_half)

    copies[2].wait()
    copies[3].wait()
    for i in (1, 3, 2):
        factor_y(i, along_y(i)).wait()
    share(fy_all, 0, core).start()
    loop(1, n_gx // 2, lambda i: factor_x(i, lax.rem(chip + i, n_gx // 2)).wait())
    share(fx_all, 1, core).start()
    share(fy_all, 0, 1 - core).wait()
    whole = (joined(p_high), joined(p_low))
    inner = split(dot3(whole, split(fy_all[...].reshape(512, 256)), ((1,), (0,))))
    share(fx_all, 1, 1 - core).wait()
    product = dot3(split(fx_all[...].reshape(512, 256)), inner, ((0,), (0,)))
    product = product.reshape(n_gx, 2, 8, 256)
    upper, lower = product[:, 0].reshape(128, 256), product[:, 1].reshape(128, 256)
    lane = lax.broadcasted_iota(jnp.int32, (128, 128), 1)
    for g in range(n_gy):
        j = g // 2 * 128
        left, right = upper[:, j : j + 128], lower[:, j : j + 128]
        if g % 2 == 0:
            right = pltpu.roll(right, 64, 1)
        else:
            left = pltpu.roll(left, 64, 1)
        tiles[g] = jnp.where(lane < 64, left, right)

    def out1(i, slot):
        t = along_y(i)
        return remote(tiles.at[t], mid.at[slot], sc1.at[i], rc1.at[slot], {"gy": t})

    for i in ORDER:
        out1(i, gy).start()
    mine1 = pltpu.make_async_copy(tiles.at[gy], mid.at[gy], local.at[0])
    mine1.start()

    def x_piece(steps, slot, h):
        to_x, to_y = step(x, steps[0]), step(y, steps[1])
        src = part1.at[h, (lax.rem(to_y, 2) * 4 + to_x) * 2 + to_y // 2]
        return remote(src, got2.at[h, slot], s2.at[h], r2.at[h], chip_at(to_x, to_y, gy))

    def y_piece(steps, slot, h):
        to_z, to_y = step(gy, steps[0]), step(y, steps[1])
        return remote(part1.at[h, to_z * 4 + to_y], got2.at[h, slot], s2.at[h], r2.at[h], chip_at(x, to_y, to_z))

    def pieces(h):
        return bytes_of(got2.at[h, pl.ds(0, 15)], s2.at[h], r2.at[h])

    def to_plane(k, slot, h):
        to_x, to_y = step(x, FAR_PAIRS[k][0]), step(y, FAR_PAIRS[k][1])
        dst = gram_y_t.at[slot, pl.ds(16 * h, 16)]
        return remote(dst, dst, s4.at[h, k], r4.at[h, slot], chip_at(to_x, to_y, gy))

    def sum_parts(part, own, h):
        for i in (1, 3, 2):
            part(i, step(own, i), h).wait()
        return (total[own, h] + got1[step(own, 2), h]) + (got1[step(own, 1), h] + got1[step(own, 3), h])

    @pl.when(core == 0)
    def _():
        for h in range(2):
            rows = sum_parts(x_part, gy, h)
            rows = jnp.concatenate([rows[:, 0:256], rows[:, 256:512]], axis=0).reshape(8, 2, 8, 256)
            even, odd = rows[:, 0].reshape(64, 256), rows[:, 1].reshape(64, 256)
            sub = lax.rem(lax.broadcasted_iota(jnp.int32, (64, 256), 0), 8)
            low = jnp.where(sub < 4, even, pltpu.roll(odd, 4, 0)).reshape(8, 8, 256)
            high = jnp.where(sub < 4, pltpu.roll(even, 60, 0), odd).reshape(8, 8, 256)
            by_tile = part1.reshape(2, 8, 2, 2, 8, 128)
            for t in range(2):
                by_tile[h, :, 0, t] = low[:, :, 128 * t : 128 * t + 128]
                by_tile[h, :, 1, t] = high[:, :, 128 * t : 128 * t + 128]
            me = x * 4 + y
            for steps in FAR_PAIRS:
                x_piece(steps, me, h).start()

    @pl.when(core == 1)
    def _():
        for h in range(2):
            rows = sum_parts(y_part, x, h)
            for z in range(4):
                part1[h, 4 * z : 4 * z + 4] = rows[:, 128 * z : 128 * z + 128].reshape(4, 16, 128)
            me = gy * 4 + y
            for steps in FAR_PAIRS:
                y_piece(steps, me, h).start()

    mine1.wait()
    for i in (1, 3, 2):
        out1(i, along_y(i)).wait()
    mid4 = mid.reshape(n_gy, n_gx, 8, 128)

    for steps in FAR_FIRST:
        t = near(steps)
        remote(mid4.at[:, t], core_tiles.at[gx], sc2.at[0], rc2.at[0], {"gx": t}).start()
    mine2 = pltpu.make_async_copy(mid4.at[:, gx], core_tiles.at[gx], local.at[1])
    mine2.start()

    to_sibling = remote(part2, last, s4.at[0, 15], r4.at[0, 16], sibling)
    all_rows = remote(gram_y_t, gram_y_t, s4.at[0, 15], r4.at[0, 17], sibling)

    def hand_over(j, h):
        rows = gram_y_t.at[j, pl.ds(16 * h, 16)]
        return remote(rows, rows, s4.at[0, 15], r4.at[0, 17], sibling)


    @pl.when(core == 0)
    def _():
        me = x * 4 + y
        for h in range(2):
            pieces(h).wait()
            got2[h, me] = part1[h, (y_lo * 4 + x) * 2 + sa]
            part2[16 * h : 16 * h + 16] = jnp.sum(got2[h], axis=0) * scale
        to_sibling.start()
        for t in range(4):
            gram_x[:, 128 * t : 128 * t + 128] = part2[8 * t : 8 * t + 4]
        to_sibling.wait_send()
        all_rows.wait_recv()

    @pl.when(core == 1)
    def _():
        me = gy * 4 + y
        here = x * 4 + y
        for h in range(2):
            pieces(h).wait()
            got2[h, me] = part1[h, me]
            gram_y_t[here, 16 * h : 16 * h + 16] = jnp.sum(got2[h], axis=0) * scale
            for k in range(15):
                to_plane(k, here, h).start()
            hand_over(here, h).start()
        for h in range(2):
            for k in range(14, -1, -1):
                j = step(x, FAR_PAIRS[k][0]) * 4 + step(y, FAR_PAIRS[k][1])
                to_plane(k, j, h).wait_recv()
                hand_over(j, h).start()
        to_sibling.wait_recv()
        for t in range(4):
            gram_x[:, 128 * t : 128 * t + 128] = last[8 * t + 4 : 8 * t + 8]
        for h in range(2):
            for k in range(15):
                to_plane(k, here, h).wait_send()
        all_rows.wait_send()

    mine2.wait()
    bytes_of(core_tiles.at[pl.ds(0, 15)], sc2.at[0], rc2.at[0]).wait()
    loop(0, 4, lambda q: swap(q).wait_send())
    for p in range(2):
        three(sa1.at[p], ra1.at[p]).wait_send()
        fifteen(sb1.at[p], rb1.at[p]).wait_send()
        fifteen(sa2.at[p], ra2.at[p]).wait_send()
        three(sb2.at[p], rb2.at[p]).wait_send()


def finish_kernel(gx_in, gy_in, core_in, gx_out, gy_out, core_out):
    gx_out[...] = gx_in[...]
    gy_out[...] = gy_in[...].reshape(512, 128).T
    tile = core_in[...].reshape(64, 8, 128)
    core_out[:, 0:8, :] = tile[:, :, 0:64]
    core_out[:, 8:16, :] = tile[:, :, 64:128]


def shards(slab, factor_x, factor_y):
    z_cells, s_local, x_local, y_local = slab.shape
    n_gx, n_gy, n_sa = lax.axis_size("gx"), lax.axis_size("gy"), lax.axis_size("sa")
    scale = 1.0 / (y_local * n_gy * z_cells * s_local * n_sa)
    rank = factor_x.shape[1]
    vmem = pltpu.VMEM
    results = pl.pallas_call(
        functools.partial(tucker_kernel, scale),
        out_shape=(
            jax.ShapeDtypeStruct((4, 512), F32),
            jax.ShapeDtypeStruct((16, 32, 128), F32),
            jax.ShapeDtypeStruct((n_gx, n_gy, 8, 128), F32),
        ),
        in_specs=[HBM] * 3,
        out_specs=(VMEM,) * 3,
        scratch_shapes=[
            vmem((2, 4, 16, 8, 128), F32), vmem((2, 16, 4, 8, 128), F32), vmem((4, 16, 32, 128), F32),
            vmem((8, 2, 32, 256), F32), vmem((4, 2, 64, 256), F32),
            vmem((4, 512, 128), BF16), vmem((4, 512, 128), BF16),
            vmem((4, 128, 512), F32), vmem((4, 128, 512), F32), vmem((4, 2, 64, 512), F32), vmem((4, 2, 64, 512), F32),
            vmem((2, 16, 16, 128), F32), vmem((2, 16, 16, 128), F32), vmem((32, 128), F32), vmem((32, 128), F32),
            vmem((4, 128, 128), F32), vmem((4, 128, 128), F32),
            DMA((2,)), DMA((2,)), DMA((2,)), DMA((2,)), DMA((2,)), DMA((2,)), DMA((2,)), DMA((2,)),
            DMA((8,)), DMA((8,)), DMA((4,)), DMA((4,)), DMA((2,)), DMA((2,)),
            DMA((4,)), DMA((4,)), DMA((4, 2)), DMA((4, 2)), DMA((2,)), DMA((2,)), DMA((2, 16)), DMA((2, 18)),
            DMA((4,)), DMA((4,)), DMA((16,)), DMA((16,)), DMA((10,)),
        ],
        compiler_params=pltpu.CompilerParams(collective_id=0, has_side_effects=True, vmem_limit_bytes=40 << 20),
        name="tucker",
    )(
        *(pltpu.with_memory_space_constraint(v, pltpu.HBM) for v in (
            slab.reshape(n_gx, n_gy, x_local, y_local), factor_x, factor_y.reshape(2, y_local // 2, rank)))
    )
    gram_x, gram_y, core = pl.pallas_call(
        finish_kernel,
        out_shape=(
            jax.ShapeDtypeStruct((4, 512), F32),
            jax.ShapeDtypeStruct((128, 512), F32),
            jax.ShapeDtypeStruct((64, 16, 64), F32),
        ),
        in_specs=[VMEM] * 3,
        out_specs=(VMEM,) * 3,
        compiler_params=pltpu.CompilerParams(vmem_limit_bytes=40 << 20),
        name="finish",
    )(*results)
    return gram_x, gram_y, core.reshape(z_cells, s_local, rank // n_gx, rank // n_gy)


def solution(mesh):
    in_specs = (P(None, "sa", "gx", "gy"), P("gx", None), P("gy", None))
    out_specs = (P(("gx", "gy", "sa"), None), P("gy", None), P(None, "sa", "gx", "gy"))
    return jax.shard_map(shards, mesh=mesh, in_specs=in_specs, out_specs=out_specs, check_vma=False)
```
